32 devices in a mesh: fsdp: 8 (over z, y), ctx: 2 (over x), tp: 2 (over core).
Axes of the slice: x: 2, y: 2, z: 4, core: 2. Of those that a mesh axis runs over, the one named last changes fastest.
Arguments:
- tokens: bfloat16 [8, 2, 1280, 768], P('fsdp', 'ctx'), may hold values from -6 to 6
- cotangent: bfloat16 [8, 2, 1280, 768], P('fsdp', 'ctx'), may hold values from -6 to 6
- routes: int32 [8, 2, 1280, 1], P('fsdp', 'ctx', 'tp'), may hold values from 0 to 15; in each aligned block of 640 rows (0 to 639, 640 to 1279, ..., all dimensions but the last counted through in order) at most 80 rows name the same one
- qkv_weight: bfloat16 [3, 768, 768], P(None, 'fsdp', 'tp'), may hold values from -0.3125 to 0.3125
- out_weight: bfloat16 [768, 768], P('tp', 'fsdp'), may hold values from -0.625 to 0.625
- layer_norm_gains: float32 [2, 768], replicated, may hold values from 0.5 to 1.5
- layer_norm_biases: float32 [2, 768], replicated, may hold values from -2 to 2
- up_weight: bfloat16 [16, 768, 3072], P('fsdp', ('ctx', 'tp')), may hold values from -0.21875 to 0.21875
- up_shift: bfloat16 [16, 3072], P('fsdp', ('ctx', 'tp')), may hold values from -2 to 2
- down_weight: bfloat16 [16, 3072, 768], P('fsdp', ('ctx', 'tp')), may hold values from -0.3125 to 0.3125
- down_shift: bfloat16 [16, 768], P('fsdp', ('ctx', 'tp')), may hold values from -2 to 2
- centroids: bfloat16 [16, 768], P('fsdp', ('ctx', 'tp')), may hold values from -0.15625 to 0.15625
Outputs:
- mixed: bfloat16 [8, 2, 1280, 768], P('fsdp', 'ctx')
- tokens_grad: float32 [8, 2, 1280, 768], P('fsdp', 'ctx')
- qkv_grad: float32 [3, 768, 768], P(None, ('fsdp', 'ctx'), 'tp')
- out_grad: float32 [768, 768], P('tp', ('fsdp', 'ctx'))
- gains_grad: float32 [2, 768], P(None, ('fsdp', 'ctx'))
- shifts_grad: float32 [2, 768], P(None, ('fsdp', 'ctx'))
- up_grad: float32 [16, 768, 3072], P('fsdp', ('ctx', 'tp'))
- up_shift_grad: float32 [16, 3072], P('fsdp', ('ctx', 'tp'))
- down_grad: float32 [16, 3072, 768], P('fsdp', ('ctx', 'tp'))
- down_shift_grad: float32 [16, 768], P('fsdp', ('ctx', 'tp'))
- centroids_grad: float32 [16, 768], P('fsdp', ('ctx', 'tp'))
The draws below stay inside these ranges and needn't reach their ends.
Inputs may be any that keep to these rules, and one draw needn't show every extreme that they name: `routes`: in each aligned block of 640 tokens (the tokens of dimension 2 taken in halves of a block, in order), no expert is named more than 80 times, a bound that some block reaches.
All inputs are finite; a program needn't handle non-finite values.
Results may differ from the reference program's by a relative error of at most 0.024.
Values may be sent and summed in bfloat16 or wider, within the bound.
No kernel may reach another device: no remote copies, remote signals or barrier semaphores. Data moves between devices by JAX's collectives and lax.ppermute only.
A program may use at most 256 MiB of HBM per device.

```python
import math
from functools import partial
import jax
import jax.numpy as jnp
import numpy as np
from jax import lax

D = 768
HEADS = 12
HEAD_DIM = 64
FF = 3072
PROMPT = 2048
LEN = 256
CTXS = 2
GROUPS = 8
PSLICE = 1024
BLOCK = 1280
ROWS = 640
TOKENS = 20480
EXPERTS = 16
CAP = 80


def block_scale(own_key, extent, shards, low, top_value):
    level, own = 1.0, jax.random.fold_in(own_key, 6)
    for axis_at, blocks in shards:
        draws = jnp.exp(jax.random.uniform(jax.random.fold_in(own, axis_at), (blocks,), jnp.float32, low / len(shards), top_value / len(shards)))
        level = level * jnp.repeat(draws, extent[axis_at] // blocks).reshape([-1 if axis == axis_at else 1 for axis in range(len(extent))])
    return level


def routed_block(key, own, number, rows, amount, top, most, skew):
    order = jax.random.permutation(key, amount)
    crowded, usual = portions_of(amount, rows * top, most, skew, True), portions_of(amount, rows * top, most, skew, False)
    places = jnp.arange(amount)

    def named(sizes, rotation):
        used = int((sizes > 0).sum())
        fixed = max(1, used // 4)
        shifted = fixed + (places - fixed + rotation * (used - fixed)) % max(1, amount - fixed)
        return jnp.zeros((amount,), jnp.int32).at[order[jnp.where(places < fixed, places, shifted)]].set(jnp.asarray(sizes, jnp.int32))

    sizes = jnp.where(number % 4 == 0, named(crowded, number // 4), named(usual, number - number // 4 - 1))
    mixed = jax.random.permutation(jax.random.fold_in(own, 3), amount)
    donor, sink = mixed[0:amount // 2 * 2:2], mixed[1:amount // 2 * 2:2]
    margin = jnp.minimum(sizes[donor] - 1, most - sizes[sink]) // 2
    margin = jnp.where((donor == order[0]) | (sink == order[0]) | (sizes[sink] == 0), 0, jnp.maximum(margin, 0))
    shifted = jax.random.randint(jax.random.fold_in(own, 4), (amount // 2,), 0, 1 << 20) % (margin + 1)
    sizes = sizes.at[donor].add(-shifted).at[sink].add(shifted)
    labels = jnp.searchsorted(jnp.cumsum(sizes), jnp.arange(rows * top), side="right").astype(jnp.int32)
    listing = labels.reshape(top, rows).T
    listing = listing[jax.random.permutation(jax.random.fold_in(own, 1), rows)]
    rotation = jax.random.randint(jax.random.fold_in(own, 2), (rows, 1), 0, top)
    return jnp.take_along_axis(listing, (jnp.arange(top)[None, :] + rotation) % top, axis=1)


def portions_of(count, total, bound, skew, full):
    loads = [(1 << 20) // math.isqrt(grade ** skew) + 1 for grade in range(1, count + 1)]
    largest = bound if full else min(bound, max(-(-total // count), total * loads[0] // sum(loads)))
    least = 1 if total - largest >= count - 1 else 0
    holding, rest = [largest] + [least] * (count - 1), total - largest - least * (count - 1)
    while rest > 0:
        candidates = [i for i in range(1, count) if holding[i] < largest] or [i for i in range(1, count) if holding[i] < bound]
        pool, left = sum([loads[i] for i in candidates]), rest
        for i in candidates:
            addition = min(bound - holding[i], max(1, left * loads[i] // pool), rest)
            holding[i] = holding[i] + addition
            rest = rest - addition
    return np.array(holding)


def normal_values(own_key, dims, scale, limit, shards=(), held_as=jnp.bfloat16):
    factor_of = block_scale(own_key, dims, shards, -0.22, 0.18) if shards else 1.0
    values = jax.random.normal(own_key, dims, jnp.float32) * scale * factor_of
    return jnp.minimum(jnp.maximum(values, -limit), limit).astype(held_as)


def setup_inputs(seed: int = 0) -> dict:
    arg_keys = jax.random.split(jax.random.key(seed), 13)
    tokens = normal_values(arg_keys[0], (GROUPS, CTXS, BLOCK, D), 1.0, 6.0, ((0, 8), (1, 2)))
    cotangent = normal_values(arg_keys[1], (GROUPS, CTXS, BLOCK, D), 1.0, 6.0, ((0, 8), (1, 2)))
    routes_keys = jax.random.split(jax.random.fold_in(arg_keys[2], 1), GROUPS * CTXS * BLOCK // ROWS)
    routes_turns = jax.random.permutation(jax.random.fold_in(arg_keys[2], 3), GROUPS * CTXS * BLOCK // ROWS)
    routes = jax.vmap(lambda own, number: routed_block(jax.random.fold_in(arg_keys[2], 2), own, number, ROWS, EXPERTS, 1, CAP, 1))(routes_keys, routes_turns).reshape((GROUPS, CTXS, BLOCK, 1))
    qkv_weight = normal_values(arg_keys[3], (3, D, D), (D // 2) ** -0.5, 0.3125, ((1, 8), (2, 2)))
    out_weight = normal_values(arg_keys[4], (D, D), (D // 8) ** -0.5, 0.625, ((0, 2), (1, 8)))
    layer_norm_gains = jnp.clip(1.0 + 0.1 * jax.random.normal(arg_keys[5], (2, D), jnp.float32), 0.5, 1.5)
    layer_norm_biases = normal_values(arg_keys[6], (2, D), 0.3, 2.0, (), jnp.float32)
    up_weight = normal_values(arg_keys[7], (EXPERTS, D, FF), D ** -0.5, 0.21875, ((0, 8), (1, 4)))
    up_shift = normal_values(arg_keys[8], (EXPERTS, FF), 0.3, 2.0, ((0, 8), (1, 4)))
    down_weight = normal_values(arg_keys[9], (EXPERTS, FF, D), (FF // 8) ** -0.5, 0.3125, ((0, 8), (1, 4)))
    down_shift = normal_values(arg_keys[10], (EXPERTS, D), 0.3, 2.0, ((0, 8), (1, 4)))
    centroids = normal_values(arg_keys[11], (EXPERTS, D), (2 * D) ** -0.5, 0.15625, ((0, 8), (1, 4)))
    return {"tokens": tokens, "cotangent": cotangent, "routes": routes, "qkv_weight": qkv_weight, "out_weight": out_weight, "layer_norm_gains": layer_norm_gains, "layer_norm_biases": layer_norm_biases, "up_weight": up_weight, "up_shift": up_shift, "down_weight": down_weight, "down_shift": down_shift, "centroids": centroids}


@jax.custom_vjp
def low(v):
    return lax.optimization_barrier(v.astype(jnp.bfloat16)).astype(jnp.float32)

@jax.custom_vjp
def low_back(v):
    return v

def low_keep(v):
    return (low(v), None)

def low_pass(kept, grad):
    return (grad,)

def back_keep(v):
    return (v, None)

def back_low(kept, grad):
    return (low(grad),)
low.defvjp(low_keep, low_pass)
low_back.defvjp(back_keep, back_low)
HIGH = lax.Precision.HIGHEST
EPS = 1e-05
NEG = -1e+30

def norm_input_rows(values, gain, shift):
    mean = lax.optimization_barrier(jnp.mean(values, axis=-1, keepdims=True))
    centred = values - mean
    spread = lax.rsqrt(lax.optimization_barrier(jnp.mean(centred * centred, axis=-1, keepdims=True)) + EPS)
    return centred * spread * gain + shift

def allowed_keys(place, pslice, prompt, length):
    shape = (pslice + length, prompt + length)
    rows = lax.broadcasted_iota(jnp.int32, shape, 0)
    cols = lax.broadcasted_iota(jnp.int32, shape, 1)
    prompt_row = rows < pslice
    prompt_col = cols < prompt
    early = prompt_row & prompt_col & (cols <= place * pslice + rows)
    later = jnp.logical_not(prompt_row) & (prompt_col | (cols - prompt <= rows - pslice))
    return early | later

def block_attention(place, block_queries, prompt_keys, prompt_values, own_keys, own_values):
    keys = jnp.concatenate([prompt_keys, own_keys], axis=0).reshape(PROMPT + LEN, HEADS, HEAD_DIM)
    values = jnp.concatenate([prompt_values, own_values], axis=0).reshape(PROMPT + LEN, HEADS, HEAD_DIM)
    queries = block_queries.reshape(BLOCK, HEADS, HEAD_DIM)
    scores = low_back(jnp.einsum('qhd,khd->hqk', queries, keys, precision=HIGH) * HEAD_DIM ** (-0.5))
    scores = jnp.where(allowed_keys(place, PSLICE, PROMPT, LEN)[None], scores, NEG)
    top = lax.optimization_barrier(jnp.max(scores, axis=-1, keepdims=True))
    weights = jnp.exp(scores - top)
    shares = low(weights / lax.optimization_barrier(jnp.sum(weights, axis=-1, keepdims=True)))
    context = jnp.einsum('hqk,khd->qhd', shares, values, precision=HIGH)
    return low_back(low(context.reshape(BLOCK, D)))

def group_attention(parts):
    group_queries, group_keys, group_values = parts
    prompt_keys = group_keys[:, :PSLICE].reshape(PROMPT, D)
    prompt_values = group_values[:, :PSLICE].reshape(PROMPT, D)

    def one_block(inner):
        place, block_queries, block_keys, block_values = inner
        return block_attention(place, block_queries, prompt_keys, prompt_values, block_keys[PSLICE:], block_values[PSLICE:])
    return lax.map(jax.checkpoint(one_block), (lax.iota(jnp.int32, CTXS), group_queries, group_keys, group_values))

def forward(routes, tokens, qkv_weight, out_weight, layer_norm_gains, layer_norm_biases, up_weight, up_shift, down_weight, down_shift, centroids):
    residual_stream = tokens.reshape(TOKENS, D)
    first = low(norm_input_rows(residual_stream, layer_norm_gains[0], layer_norm_biases[0]))
    queries = low_back(low(jnp.dot(first, qkv_weight[0], precision=HIGH)))
    keys = low_back(low(jnp.dot(first, qkv_weight[1], precision=HIGH)))
    values = low_back(low(jnp.dot(first, qkv_weight[2], precision=HIGH)))
    shape = (GROUPS, CTXS, BLOCK, D)
    context = lax.map(jax.checkpoint(group_attention), (queries.reshape(shape), keys.reshape(shape), values.reshape(shape)))
    attended = low_back(jnp.dot(context.reshape(TOKENS, D), out_weight, precision=HIGH))
    residual_rows = residual_stream + attended
    second = low_back(low(norm_input_rows(residual_rows, layer_norm_gains[1], layer_norm_biases[1])))
    route = routes.reshape(TOKENS).astype(jnp.int32)
    member = (route[:, None] == lax.broadcasted_iota(jnp.int32, (TOKENS, EXPERTS), 1)).astype(jnp.int32)
    rank = lax.optimization_barrier(jnp.sum((jnp.cumsum(member, axis=0).astype(jnp.int32) - 1) * member, axis=1)).astype(jnp.int32)
    most = TOKENS // ROWS * CAP
    slots = jnp.full((EXPERTS, most), TOKENS, jnp.int32).at[route, rank].set(lax.iota(jnp.int32, TOKENS))
    padded = jnp.concatenate([second, jnp.zeros((1, D), jnp.float32)], axis=0)

    def expert_rows(parts):
        index, w_up, b_up, w_down, b_down, centre = parts
        rows = padded[index]
        gate = jax.nn.sigmoid(low_back(jnp.dot(rows, centre, precision=HIGH)))
        inner = low_back(jnp.dot(rows, w_up, precision=HIGH) + b_up)
        hidden = low(jax.nn.gelu(inner, approximate=False))
        result = low_back(jnp.dot(hidden, w_down, precision=HIGH) + b_down)
        return low_back(low(gate[:, None] * result))
    expert_out = lax.map(jax.checkpoint(expert_rows), (slots, up_weight, up_shift, down_weight, down_shift, centroids))
    gathered = expert_out.reshape(EXPERTS * most, D)[route * most + rank]
    return (residual_rows + gathered).reshape(shape)

def reference(tokens, cotangent, routes, qkv_weight, out_weight, layer_norm_gains, layer_norm_biases, up_weight, up_shift, down_weight, down_shift, centroids):
    floats = tuple((array.astype(jnp.float32) for array in (tokens, qkv_weight, out_weight, layer_norm_gains, layer_norm_biases, up_weight, up_shift, down_weight, down_shift, centroids)))
    value, pull = jax.vjp(partial(forward, routes), *floats)
    grads = pull(cotangent.astype(jnp.float32))
    return (value.astype(jnp.bfloat16), grads[0], grads[1], grads[2], grads[3], grads[4], grads[5], grads[6], grads[7], grads[8], grads[9])
```

```python
from functools import partial

import jax
import jax.numpy as jnp
from jax import lax
from jax.experimental import pallas as pl
from jax.experimental.pallas import tpu as pltpu
from jax.sharding import PartitionSpec as P

HEAD_DIM = 64
PROMPT = 2048
LEN = 256


EPS = 1e-05
NEG = -1e30


def norm_input_rows(values, gain, shift):
    mean = jnp.mean(values, axis=-1, keepdims=True)
    centred = values - mean
    spread = lax.rsqrt(jnp.mean(centred * centred, axis=-1, keepdims=True) + EPS)
    normed = centred * spread
    return (normed * gain + shift, normed, spread)


def norm_back(upstream, normed, spread, gain):
    scaled = upstream * gain
    inner = (
        scaled
        - jnp.mean(scaled, axis=-1, keepdims=True)
        - normed * jnp.mean(scaled * normed, axis=-1, keepdims=True)
    )
    return (spread * inner, jnp.sum(upstream * normed, axis=0), jnp.sum(upstream, axis=0))


def allowed_keys(place, pslice, prompt, length):
    shape = (pslice + length, prompt + length)
    rows = lax.broadcasted_iota(jnp.int32, shape, 0)
    cols = lax.broadcasted_iota(jnp.int32, shape, 1)
    prompt_row = rows < pslice
    prompt_col = cols < prompt
    early = prompt_row & prompt_col & (cols <= place * pslice + rows)
    later = jnp.logical_not(prompt_row) & (prompt_col | (cols - prompt <= rows - pslice))
    return early | later


def dense_weights(qkv_weight, out_weight):
    return (
        lax.all_gather(qkv_weight, "fsdp", axis=1, tiled=True),
        lax.all_gather(out_weight, "fsdp", axis=1, tiled=True),
    )


def expert_weights(up_weight, down_weight, up_shift, down_shift, centroids):
    return (
        lax.all_gather(up_weight, ("ctx", "tp"), axis=1, tiled=True),
        lax.all_gather(down_weight, ("ctx", "tp"), axis=1, tiled=True),
        lax.all_gather(up_shift, ("ctx", "tp"), axis=1, tiled=True),
        lax.all_gather(down_shift, ("ctx", "tp"), axis=1, tiled=True),
        lax.all_gather(centroids, ("ctx", "tp"), axis=1, tiled=True),
    )


def tp_rows(rows):
    return lax.all_gather(rows, "tp", axis=0, tiled=True)


def head_total(terms):
    return lax.psum(terms.astype(jnp.bfloat16), "tp").astype(jnp.float32)


def split_heads(matrix):
    return matrix.reshape(matrix.shape[0], -1, HEAD_DIM).transpose(1, 0, 2)


def join_heads(stacked):
    return stacked.transpose(1, 0, 2).reshape(stacked.shape[1], -1)


def head_forward(allowed, scale, parts):
    query, keys, values = parts
    raw = jnp.einsum("qd,kd->qk", query, keys, preferred_element_type=jnp.float32) * scale
    scores = jnp.where(allowed, raw, NEG)
    top = jnp.max(scores, axis=-1, keepdims=True)
    weights = jnp.exp(scores - top)
    total = jnp.sum(weights, axis=-1, keepdims=True)
    shares = (weights / total).astype(jnp.bfloat16)
    context = jnp.dot(shares, values, preferred_element_type=jnp.float32).astype(jnp.bfloat16)
    return (context, (top + jnp.log(total))[:, 0])


def head_backward(allowed, scale, parts):
    query, keys, values, context_grad, log_total = parts
    raw = jnp.einsum("qd,kd->qk", query, keys, preferred_element_type=jnp.float32) * scale
    scores = jnp.where(allowed, raw, NEG)
    weights = jnp.exp(scores - log_total[:, None])
    values_grad = jnp.einsum(
        "qk,qd->kd", weights.astype(jnp.bfloat16), context_grad, preferred_element_type=jnp.float32
    )
    weight_grad = jnp.einsum("qd,kd->qk", context_grad, values, preferred_element_type=jnp.float32)
    row_dot = jnp.sum(weights * weight_grad, axis=-1, keepdims=True)
    logit_grad = (weights * (weight_grad - row_dot)).astype(jnp.bfloat16)
    query_grad = jnp.dot(logit_grad, keys, preferred_element_type=jnp.float32) * scale
    keys_grad = (
        jnp.einsum("qk,qd->kd", logit_grad, query, preferred_element_type=jnp.float32) * scale
    )
    return (query_grad, keys_grad, values_grad)


def shards_any(
    tokens,
    cotangent,
    routes,
    qkv_weight,
    out_weight,
    layer_norm_gains,
    layer_norm_biases,
    up_weight,
    up_shift,
    down_weight,
    down_shift,
    centroids,
):
    block = tokens.shape[2]
    width = tokens.shape[3]
    pslice = block - LEN
    half = routes.shape[2]
    place = lax.axis_index("ctx")
    half_start = lax.axis_index("tp") * half
    scale = HEAD_DIM ** (-0.5)
    residual_stream = tokens.reshape(block, width).astype(jnp.float32)
    project_full, output_full = dense_weights(qkv_weight, out_weight)
    first_normed_rows, first_standardized, first_deviation = norm_input_rows(
        residual_stream, layer_norm_gains[0], layer_norm_biases[0]
    )
    first = first_normed_rows.astype(jnp.bfloat16)
    projected = jnp.einsum(
        "rd,jde->jre", first, project_full, preferred_element_type=jnp.float32
    ).astype(jnp.bfloat16)
    queries, keys_own, values_own = (projected[0], projected[1], projected[2])
    prompt_keys, prompt_values = (
        lax.all_gather(keys_own[:pslice], "ctx", axis=0, tiled=True),
        lax.all_gather(values_own[:pslice], "ctx", axis=0, tiled=True),
    )
    keys_all = jnp.concatenate([prompt_keys, keys_own[pslice:]], axis=0)
    values_all = jnp.concatenate([prompt_values, values_own[pslice:]], axis=0)
    allowed = allowed_keys(place, pslice, PROMPT, LEN)
    query_heads = split_heads(queries)
    key_heads = split_heads(keys_all)
    value_heads = split_heads(values_all)
    context_heads, log_total = lax.map(
        partial(head_forward, allowed, scale), (query_heads, key_heads, value_heads)
    )
    context = join_heads(context_heads)
    attended = head_total(jnp.dot(context, output_full, preferred_element_type=jnp.float32))
    residual_rows = residual_stream + attended
    second_normed_rows, second_standardized, second_deviation = norm_input_rows(
        residual_rows, layer_norm_gains[1], layer_norm_biases[1]
    )
    second = second_normed_rows.astype(jnp.bfloat16)
    own_rows = lax.dynamic_slice_in_dim(second, half_start, half, 0)
    route = routes.reshape(half)
    local_experts = up_weight.shape[0]
    owners = lax.axis_size("fsdp")
    total_experts = local_experts * owners
    capacity = 2 * half // total_experts
    slots = total_experts * capacity
    member = (route[:, None] == lax.broadcasted_iota(jnp.int32, (half, total_experts), 1)).astype(
        jnp.int32
    )
    rank = jnp.sum((jnp.cumsum(member, axis=0) - 1) * member, axis=1)
    slot_of = route * capacity + rank
    placing = (lax.broadcasted_iota(jnp.int32, (slots, half), 0) == slot_of[None, :]).astype(
        jnp.bfloat16
    )
    outgoing = (
        jnp.dot(placing, own_rows, preferred_element_type=jnp.float32)
        .astype(jnp.bfloat16)
        .reshape(owners, local_experts, capacity, width)
    )
    up_full, down_full, up_bias, down_bias, centres = expert_weights(
        up_weight, down_weight, up_shift, down_shift, centroids
    )
    arrived = lax.all_to_all(outgoing, "fsdp", split_axis=0, concat_axis=0, tiled=True)
    score = jnp.einsum("sekd,ed->sek", arrived, centres, preferred_element_type=jnp.float32)
    gate = jax.nn.sigmoid(score)
    inner = jnp.einsum(
        "sekd,edf->sekf", arrived, up_full, preferred_element_type=jnp.float32
    ) + up_bias[None, :, None, :].astype(jnp.float32)
    hidden = jax.nn.gelu(inner, approximate=False).astype(jnp.bfloat16)
    result = jnp.einsum(
        "sekf,efd->sekd", hidden, down_full, preferred_element_type=jnp.float32
    ) + down_bias[None, :, None, :].astype(jnp.float32)
    sent = (gate[..., None] * result).astype(jnp.bfloat16)
    returned = lax.all_to_all(sent, "fsdp", split_axis=0, concat_axis=0, tiled=True)
    returned, arrived, inner, hidden, gate, result = (
        returned,
        arrived,
        inner,
        hidden,
        gate,
        result,
    )
    back_rows = jnp.einsum(
        "sr,sd->rd", placing, returned.reshape(slots, width), preferred_element_type=jnp.float32
    ).astype(jnp.bfloat16)
    expert_out = tp_rows(back_rows)
    mixed = (residual_rows + expert_out.astype(jnp.float32)).astype(jnp.bfloat16)
    project_back, output_back = dense_weights(qkv_weight, out_weight)
    up_back, down_back, unused_up, unused_down, centre_back = expert_weights(
        up_weight, down_weight, up_shift, down_shift, centroids
    )
    upstream_rows = cotangent.reshape(block, width)
    upstream = upstream_rows.astype(jnp.float32)
    upstream_half = lax.dynamic_slice_in_dim(upstream_rows, half_start, half, 0)
    grad_out = (
        jnp.dot(placing, upstream_half, preferred_element_type=jnp.float32)
        .astype(jnp.bfloat16)
        .reshape(owners, local_experts, capacity, width)
    )
    arrived_grad = lax.all_to_all(grad_out, "fsdp", split_axis=0, concat_axis=0, tiled=True).astype(
        jnp.float32
    )
    result_grad = (gate[..., None] * arrived_grad).astype(jnp.bfloat16)
    gate_grad = jnp.sum(arrived_grad * result, axis=-1)
    score_grad = (gate_grad * gate * (1.0 - gate)).astype(jnp.bfloat16)
    hidden_grad = jnp.einsum(
        "sekd,efd->sekf", result_grad, down_back, preferred_element_type=jnp.float32
    )
    gelu_pull = jax.vjp(partial(jax.nn.gelu, approximate=False), inner)[1]
    inner_grad = gelu_pull(hidden_grad)[0].astype(jnp.bfloat16)
    rows_grad = jnp.einsum(
        "sekf,edf->sekd", inner_grad, up_back, preferred_element_type=jnp.float32
    )
    rows_grad = rows_grad + score_grad.astype(jnp.float32)[..., None] * centre_back[
        None, :, None, :
    ].astype(jnp.float32)
    sent_grad = lax.all_to_all(
        rows_grad.astype(jnp.bfloat16), "fsdp", split_axis=0, concat_axis=0, tiled=True
    )
    up_local = jnp.einsum("sekd,sekf->edf", arrived, inner_grad, preferred_element_type=jnp.float32)
    down_local = jnp.einsum(
        "sekf,sekd->efd", hidden, result_grad, preferred_element_type=jnp.float32
    )
    up_shift_local = jnp.sum(inner_grad.astype(jnp.float32), axis=(0, 2))
    down_shift_local = jnp.sum(result_grad.astype(jnp.float32), axis=(0, 2))
    centre_local = jnp.einsum(
        "sek,sekd->ed", score_grad, arrived, preferred_element_type=jnp.float32
    )
    up_grad, down_grad, up_shift_grad, down_shift_grad, centroids_grad = (
        lax.psum_scatter(
            up_local.astype(jnp.bfloat16), ("ctx", "tp"), scatter_dimension=1, tiled=True
        ).astype(jnp.float32),
        lax.psum_scatter(
            down_local.astype(jnp.bfloat16), ("ctx", "tp"), scatter_dimension=1, tiled=True
        ).astype(jnp.float32),
        lax.psum_scatter(
            up_shift_local.astype(jnp.bfloat16), ("ctx", "tp"), scatter_dimension=1, tiled=True
        ).astype(jnp.float32),
        lax.psum_scatter(
            down_shift_local.astype(jnp.bfloat16), ("ctx", "tp"), scatter_dimension=1, tiled=True
        ).astype(jnp.float32),
        lax.psum_scatter(
            centre_local.astype(jnp.bfloat16), ("ctx", "tp"), scatter_dimension=1, tiled=True
        ).astype(jnp.float32),
    )
    half_grad = jnp.einsum(
        "sr,sd->rd", placing, sent_grad.reshape(slots, width), preferred_element_type=jnp.float32
    ).astype(jnp.bfloat16)
    second_norm_gradient = tp_rows(half_grad).astype(jnp.float32)
    resid_norm_grad, gain_two_grad, shift_two_grad = norm_back(
        second_norm_gradient, second_standardized, second_deviation, layer_norm_gains[1]
    )
    resid_grad = upstream + resid_norm_grad
    attended_grad = resid_grad.astype(jnp.bfloat16)
    output_grad = jnp.einsum(
        "rh,rd->hd", context, attended_grad, preferred_element_type=jnp.float32
    )
    context_grad = jnp.einsum(
        "rd,hd->rh", attended_grad, output_back, preferred_element_type=jnp.float32
    ).astype(jnp.bfloat16)
    query_grad, keys_grad, values_grad = lax.map(
        partial(head_backward, allowed, scale),
        (query_heads, key_heads, value_heads, split_heads(context_grad), log_total),
    )
    keys_flat = join_heads(keys_grad)
    values_flat = join_heads(values_grad)
    prompt_key_grad, prompt_value_grad = (
        lax.psum_scatter(
            keys_flat[:PROMPT].astype(jnp.bfloat16), "ctx", scatter_dimension=0, tiled=True
        ).astype(jnp.float32),
        lax.psum_scatter(
            values_flat[:PROMPT].astype(jnp.bfloat16), "ctx", scatter_dimension=0, tiled=True
        ).astype(jnp.float32),
    )
    keys_total = jnp.concatenate([prompt_key_grad, keys_flat[PROMPT:]], axis=0).astype(jnp.bfloat16)
    values_total = jnp.concatenate([prompt_value_grad, values_flat[PROMPT:]], axis=0).astype(
        jnp.bfloat16
    )
    queries_total = join_heads(query_grad).astype(jnp.bfloat16)
    stacked = jnp.stack([queries_total, keys_total, values_total])
    project_grad = jnp.einsum("rd,jre->jde", first, stacked, preferred_element_type=jnp.float32)
    first_norm_gradient = head_total(
        jnp.einsum("jre,jde->rd", stacked, project_back, preferred_element_type=jnp.float32)
    )
    stream_norm_grad, gain_one_grad, shift_one_grad = norm_back(
        first_norm_gradient, first_standardized, first_deviation, layer_norm_gains[0]
    )
    tokens_grad = resid_grad + stream_norm_grad
    gains_local = jnp.stack([gain_one_grad, gain_two_grad])
    shifts_local = jnp.stack([shift_one_grad, shift_two_grad])
    qkv_grad, out_grad, gains_grad, shifts_grad = (
        lax.psum_scatter(project_grad, ("fsdp", "ctx"), scatter_dimension=1, tiled=True),
        lax.psum_scatter(output_grad, ("fsdp", "ctx"), scatter_dimension=1, tiled=True),
        lax.psum_scatter(gains_local, ("fsdp", "ctx"), scatter_dimension=1, tiled=True),
        lax.psum_scatter(shifts_local, ("fsdp", "ctx"), scatter_dimension=1, tiled=True),
    )
    return (
        mixed.reshape(1, 1, block, width),
        tokens_grad.reshape(1, 1, block, width),
        qkv_grad,
        out_grad,
        gains_grad,
        shifts_grad,
        up_grad,
        up_shift_grad,
        down_grad,
        down_shift_grad,
        centroids_grad,
    )


F32=jnp.float32; BF=jnp.bfloat16
HD=64; NT=(((1,),(1,)),((),()))
TILE=256

def nt(a,b): return lax.dot_general(a,b,NT,preferred_element_type=F32)
def mm(a,b): return jnp.dot(a,b,preferred_element_type=F32)
def head_masks(rows):
    lane=lax.broadcasted_iota(jnp.int32,(rows,2*HD),1)
    return (lane<HD,lane>=HD)

def self_forward(q_ref,k_ref,v_ref,o_ref,lse_ref):
    rows=q_ref.shape[0]
    lo,hi=head_masks(TILE)
    tri=lax.broadcasted_iota(jnp.int32,(TILE,TILE),1)<=lax.broadcasted_iota(jnp.int32,(TILE,TILE),0)
    for i in range(rows//TILE):
        at=pl.ds(i*TILE,TILE)
        q=q_ref[at,:]*jnp.asarray(HD**-0.5,BF)
        outs=[];lses=[]
        for mask in (lo,hi):
            qm=jnp.where(mask,q,jnp.zeros_like(q))
            diag=jnp.where(tri,nt(qm,k_ref[at,:]),-1e30)
            top=jnp.max(diag,axis=1,keepdims=True)
            if i:
                off=nt(qm,k_ref[:i*TILE,:])
                top=jnp.maximum(top,jnp.max(off,axis=1,keepdims=True))
            pd=jnp.exp(diag-top)
            total=jnp.sum(pd,axis=1,keepdims=True)
            acc=mm(pd.astype(BF),v_ref[at,:])
            if i:
                po=jnp.exp(off-top)
                total=total+jnp.sum(po,axis=1,keepdims=True)
                acc=acc+mm(po.astype(BF),v_ref[:i*TILE,:])
            outs.append(acc/total); lses.append(top+jnp.log(total))
        o_ref[at,:]=jnp.where(lo,outs[0],outs[1])
        lse_ref[at,:]=jnp.where(lo,lses[0],lses[1])

def cross_forward(place_ref,q_ref,k_ref,v_ref,o_ref,lse_ref,ctx_ref,lse_t_ref):
    rows=q_ref.shape[0]
    lo,hi=head_masks(TILE)
    def put(i,o,lse):
        at=pl.ds(i*TILE,TILE)
        ctx_ref[at,:]=o.astype(BF)
        flipped=lse.T
        lse_t_ref[0:1,at]=flipped[0:1,:]
        lse_t_ref[1:2,at]=flipped[HD:HD+1,:]
    def tile(i):
        at=pl.ds(i*TILE,TILE)
        q=q_ref[at,:]*jnp.asarray(HD**-0.5,BF)
        outs=[];lses=[]
        for mask in (lo,hi):
            s=nt(jnp.where(mask,q,jnp.zeros_like(q)),k_ref[...])
            top=jnp.max(s,axis=1,keepdims=True)
            p=jnp.exp(s-top)
            total=jnp.sum(p,axis=1,keepdims=True)
            outs.append(mm(p.astype(BF),v_ref[...])/total); lses.append(top+jnp.log(total))
        o2=jnp.where(lo,outs[0],outs[1]); l2=jnp.where(lo,lses[0],lses[1])
        o1=o_ref[at,:]; l1=lse_ref[at,:]
        top=jnp.maximum(l1,l2)
        e1=jnp.exp(l1-top); e2=jnp.exp(l2-top)
        both=e1+e2
        put(i,(o1*e1+o2*e2)/both,top+jnp.log(both))
    own=k_ref.shape[0]//TILE
    later=place_ref[0]==1
    for i in range(rows//TILE):
        if i>=own: tile(i)
        else:
            pl.when(later)(partial(tile,i))
            @pl.when(jnp.logical_not(later))
            def _():
                at=pl.ds(i*TILE,TILE)
                put(i,o_ref[at,:],lse_ref[at,:])

def col(rows,j=None,off=0):
    if j is None: return pl.BlockSpec((rows,2*HD),lambda p,*_:(0,p))
    return pl.BlockSpec((None,rows,2*HD),lambda p,*_:(j,0,p))

def run_self_forward(qkv):
    _,rows,width=qkv.shape
    return pl.pallas_call(self_forward,grid=(width//128,),
        in_specs=[col(rows,0),col(rows,1),col(rows,2)],
        out_specs=[col(rows),col(rows)],
        out_shape=[jax.ShapeDtypeStruct((rows,width),F32)]*2,name="self_forward")(qkv,qkv,qkv)

def run_cross_forward(place,qkv,k,v,o,lse):
    _,rows,width=qkv.shape; keys=k.shape[0]
    return pl.pallas_call(cross_forward,
        grid_spec=pltpu.PrefetchScalarGridSpec(num_scalar_prefetch=1,grid=(width//128,),
        in_specs=[col(rows,0),col(keys),col(keys),col(rows),col(rows)],
        out_specs=[col(rows),pl.BlockSpec((None,2,rows),lambda p,*_:(p,0,0))]),
        out_shape=[jax.ShapeDtypeStruct((rows,width),BF),jax.ShapeDtypeStruct((width//128,2,rows),F32)],name="cross_forward")(place,qkv,k,v,o,lse)

def row_dots(g,o):
    prod=(g.astype(F32)*o.astype(F32)).T
    return jnp.sum(prod[:HD],axis=0,keepdims=True),jnp.sum(prod[HD:],axis=0,keepdims=True)

def pair_back(q,g,k,v,kt,lse,dots,masks,visible):
    ps=[];ds=[];qs=[];gs=[];dq=[]
    for h in range(2):
        qm=jnp.where(masks[h],q,jnp.zeros_like(q)); gm=jnp.where(masks[h],g,jnp.zeros_like(g))
        s=nt(k,qm)
        p=jnp.exp(s-lse[h])
        if visible is not None: p=jnp.where(visible,p,0.0)
        dp=nt(v,gm)
        d=(p*(dp-dots[h])).astype(BF)
        ps.append(p.astype(BF)); ds.append(d); qs.append(qm); gs.append(gm)
        dq.append(mm(kt[h*HD:(h+1)*HD,:],d))
    dv=mm(jnp.concatenate(ps,axis=1),jnp.concatenate(gs,axis=0))
    dk=mm(jnp.concatenate(ds,axis=1),jnp.concatenate(qs,axis=0))
    return jnp.concatenate(dq,axis=0),dk,dv

def cross_backward(place_ref,q_ref,k_ref,v_ref,g_ref,c_ref,lse_ref,dq_ref,dk_ref,dv_ref,dk_acc,dv_acc):
    rows=q_ref.shape[0]
    masks=head_masks(TILE)
    keys=k_ref.shape[0]
    dk_acc[...]=jnp.zeros_like(dk_acc); dv_acc[...]=jnp.zeros_like(dv_acc)
    kt=k_ref[...].T
    def tile(i):
        at=pl.ds(i*TILE,TILE)
        q=q_ref[at,:]*jnp.asarray(HD**-0.5,BF); g=g_ref[at,:]
        dots=row_dots(g,c_ref[at,:])
        lse=(lse_ref[0:1,at],lse_ref[1:2,at])
        dq,dk,dv=pair_back(q,g,k_ref[...],v_ref[...],kt,lse,dots,masks,None)
        dq_ref[:,at]=dq; dk_acc[...]+=dk; dv_acc[...]+=dv
    later=place_ref[0]==1
    for i in range(rows//TILE):
        if i>=keys//TILE: tile(i)
        else:
            pl.when(later)(partial(tile,i))
            @pl.when(jnp.logical_not(later))
            def _(): dq_ref[:,pl.ds(i*TILE,TILE)]=jnp.zeros((2*HD,TILE),F32)
    dk_ref[...]=dk_acc[...].astype(BF); dv_ref[...]=dv_acc[...].astype(BF)

def self_backward(q_ref,k_ref,v_ref,g_ref,c_ref,lse_ref,dqx_ref,dq_ref,dk_ref,dv_ref,dk_acc,dv_acc):
    rows=q_ref.shape[0]
    masks=head_masks(TILE)
    dk_acc[...]=jnp.zeros_like(dk_acc); dv_acc[...]=jnp.zeros_like(dv_acc)
    kt=k_ref[...].T
    seen=lax.broadcasted_iota(jnp.int32,(TILE,TILE),0)<=lax.broadcasted_iota(jnp.int32,(TILE,TILE),1)
    for i in range(rows//TILE):
        at=pl.ds(i*TILE,TILE)
        q=q_ref[at,:]*jnp.asarray(HD**-0.5,BF); g=g_ref[at,:]
        dots=row_dots(g,c_ref[at,:])
        lse=(lse_ref[0:1,at],lse_ref[1:2,at])
        dq,dk,dv=pair_back(q,g,k_ref[at,:],v_ref[at,:],kt[:,i*TILE:(i+1)*TILE],lse,dots,masks,seen)
        dk_acc[at,:]+=dk; dv_acc[at,:]+=dv
        if i:
            n=i*TILE
            dq2,dk,dv=pair_back(q,g,k_ref[:n,:],v_ref[:n,:],kt[:,:n],lse,dots,masks,None)
            dq=dq+dq2
            dk_acc[:n,:]+=dk; dv_acc[:n,:]+=dv
        dq_ref[at,:]=((dq+dqx_ref[:,at])*(HD**-0.5)).T.astype(BF)
    dk_ref[...]=dk_acc[...].astype(dk_ref.dtype); dv_ref[...]=dv_acc[...].astype(dv_ref.dtype)

def lse_spec(rows): return pl.BlockSpec((None,2,rows),lambda p,*_:(p,0,0))
def colt(rows): return pl.BlockSpec((2*HD,rows),lambda p,*_:(p,0))

def run_cross_backward(place,qkv,k,v,g,c,lse_t):
    _,rows,width=qkv.shape; keys=k.shape[0]
    return pl.pallas_call(cross_backward,
        grid_spec=pltpu.PrefetchScalarGridSpec(num_scalar_prefetch=1,grid=(width//128,),
        in_specs=[col(rows,0),col(keys),col(keys),col(rows),col(rows),lse_spec(rows)],
        out_specs=[colt(rows),col(keys),col(keys)],
        scratch_shapes=[pltpu.VMEM((keys,2*HD),F32)]*2),
        out_shape=[jax.ShapeDtypeStruct((width,rows),F32)]+[jax.ShapeDtypeStruct((keys,width),BF)]*2,name="cross_backward")(place,qkv,k,v,g,c,lse_t)

def run_self_backward(qkv,g,c,lse_t,dqx):
    _,rows,width=qkv.shape
    return pl.pallas_call(self_backward,grid=(width//128,),
        in_specs=[col(rows,0),col(rows,1),col(rows,2),col(rows),col(rows),lse_spec(rows),colt(rows)],
        out_specs=[col(rows)]*3,
        out_shape=[jax.ShapeDtypeStruct((rows,width),BF)]+[jax.ShapeDtypeStruct((rows,width),F32)]*2,
        scratch_shapes=[pltpu.VMEM((rows,2*HD),F32)]*2,name="self_backward")(qkv,qkv,qkv,g,c,lse_t,dqx)


def tn(a,b): return lax.dot_general(a,b,(((0,),(0,)),((),())),preferred_element_type=F32)
RT2=0.7071067811865476; IRT2PI=0.3989422804014327

def expert_step(order_ref,x_ref,cot_ref,up_ref,down_ref,ub_ref,db_ref,cen_ref,
                sent_ref,dx_ref,gu_ref,ku_ref,gd_ref,kd_ref,us_ref,ds_ref,cg_ref,
                rg,xt,gate,res,dx):
    j=pl.program_id(0); last=pl.num_programs(0)-1
    half=(last+1)//2
    quarter=x_ref.shape[-1]//4
    @pl.when(j==0)
    def _():
        x=x_ref[...]
        score=jnp.sum(x.astype(F32)*cen_ref[...].astype(F32),axis=1,keepdims=True)
        g=jax.nn.sigmoid(score)
        gate[...]=jnp.broadcast_to(g,gate.shape)
        r=(g*cot_ref[...].astype(F32)).astype(BF)
        rg[...]=r
        ds_ref[...]=jnp.sum(r.astype(F32),axis=0,keepdims=True)
        t=x.T
        for s in range(4):
            xt[pl.ds(order_ref[4+s]*quarter,quarter),:]=t[s*quarter:(s+1)*quarter,:]
        res[...]=jnp.zeros_like(res); dx[...]=jnp.zeros_like(dx)
    x=x_ref[...]; r=rg[...]
    inner=mm(x,up_ref[...])+ub_ref[...].astype(F32)
    cdf=0.5*(1.0+lax.erf(inner*RT2))
    hidden=(inner*cdf).astype(BF)
    slope=cdf+inner*(jnp.exp(-0.5*inner*inner)*IRT2PI)
    res[...]+=mm(hidden,down_ref[...])
    back=(nt(r,down_ref[...])*slope).astype(BF)
    us_ref[...]=jnp.sum(back.astype(F32),axis=0,keepdims=True)
    dx[...]+=nt(back,up_ref[...])
    du=mm(xt[...],back)
    gu_ref[...]=du[:2*quarter].astype(BF)
    ku_ref[...]=du[2*quarter:].astype(BF)
    dd=tn(hidden,r).astype(BF)
    @pl.when(j<half)
    def _(): gd_ref[...]=dd
    @pl.when(j>=half)
    def _(): kd_ref[...]=dd
    @pl.when(j==last)
    def _():
        g=gate[:,:1]
        out=res[...]+db_ref[...].astype(F32)
        sent_ref[...]=(g*out).astype(BF)
        sg=(jnp.sum(cot_ref[...].astype(F32)*out,axis=1,keepdims=True)*g*(1.0-g)).astype(BF).astype(F32)
        dx_ref[...]=(dx[...]+sg*cen_ref[...].astype(F32)).astype(BF)
        cg_ref[...]=jnp.sum(sg*x_ref[...].astype(F32),axis=0,keepdims=True)

def run_expert(e,order,x,cot,up,down,up_bias,down_bias,centres):
    n,w=x.shape; ff=up.shape[2]; c=ff//4
    whole=lambda r,k: pl.BlockSpec((r,k),lambda j,o:(0,0))
    return pl.pallas_call(expert_step,
      grid_spec=pltpu.PrefetchScalarGridSpec(num_scalar_prefetch=1,grid=(4,),
        in_specs=[whole(n,w),whole(n,w),
          pl.BlockSpec((None,w,c),lambda j,o:(e,0,o[j])),
          pl.BlockSpec((None,c,w),lambda j,o:(e,o[j],0)),
          pl.BlockSpec((None,1,c),lambda j,o:(e,0,o[j])),
          pl.BlockSpec((None,1,w),lambda j,o:(e,0,0)),
          pl.BlockSpec((None,1,w),lambda j,o:(e,0,0))],
        out_specs=[whole(n,w),whole(n,w),
          pl.BlockSpec((w//2,c),lambda j,o:(0,o[j])),
          pl.BlockSpec((w//2,c),lambda j,o:(0,o[j])),
          pl.BlockSpec((None,c,w),lambda j,o:(jnp.minimum(j,1),0,0)),
          pl.BlockSpec((None,c,w),lambda j,o:(jnp.maximum(j,2)-2,0,0)),
          pl.BlockSpec((1,c),lambda j,o:(0,o[j])),
          whole(1,w),whole(1,w)],
        scratch_shapes=[pltpu.VMEM((n,w),BF),pltpu.VMEM((w,n),BF),pltpu.VMEM((n,128),F32),pltpu.VMEM((n,w),F32),pltpu.VMEM((n,w),F32)]),
      out_shape=[jax.ShapeDtypeStruct((n,w),BF)]*2+[jax.ShapeDtypeStruct((w//2,ff),BF)]*2+[jax.ShapeDtypeStruct((2,c,w),BF)]*2+
        [jax.ShapeDtypeStruct((1,ff),F32),jax.ShapeDtypeStruct((1,w),F32),jax.ShapeDtypeStruct((1,w),F32)],
      name=f"expert_{e}")(order,x,cot,up,down,up_bias,down_bias,centres)


SWAP = ((0, 1), (1, 0))


def swap(value, axis):
    return lax.ppermute(value, axis, SWAP)


def join_halves(own, side):
    half = own.shape[0]
    other = swap(own, "tp")
    buffer = jnp.zeros((2 * half,) + own.shape[1:], own.dtype)
    buffer = lax.dynamic_update_slice_in_dim(buffer, own, side * half, 0)
    return lax.dynamic_update_slice_in_dim(buffer, other, (1 - side) * half, 0)


def scatter_rows(matrices, place):
    count, rows, columns = matrices.shape
    owners = lax.axis_size("fsdp")
    piece = rows // (2 * owners)
    split = matrices.reshape(count, owners, 2, piece, columns)
    give = lax.dynamic_index_in_dim(split, 1 - place, 2, keepdims=False).astype(jnp.bfloat16)
    keep = lax.dynamic_index_in_dim(split, place, 2, keepdims=False)
    total = (keep + swap(give, "ctx").astype(jnp.float32)).astype(jnp.bfloat16)
    total = total.transpose(1, 0, 2, 3)
    spread = lax.all_to_all(total, "fsdp", split_axis=0, concat_axis=0, tiled=True)
    return jnp.sum(spread.astype(jnp.float32), axis=0)


def quarter_sums(give, keep):
    received = [swap(part, "tp") for part in give]
    sends = [
        (k[0].astype(jnp.float32) + r[0].astype(jnp.float32)).astype(jnp.bfloat16)
        for k, r in zip(keep, received)
    ]
    crossed = [swap(part, "ctx") for part in sends]
    return jnp.stack(
        [
            k[1].astype(jnp.float32) + r[1].astype(jnp.float32) + c.astype(jnp.float32)
            for k, r, c in zip(keep, received, crossed)
        ]
    )


def shards_pair(
    tokens,
    cotangent,
    routes,
    qkv_weight,
    out_weight,
    layer_norm_gains,
    layer_norm_biases,
    up_weight,
    up_shift,
    down_weight,
    down_shift,
    centroids,
):
    block = tokens.shape[2]
    width = tokens.shape[3]
    pslice = block - LEN
    half = routes.shape[2]
    experts, _, ff = up_weight.shape
    owners = lax.axis_size("fsdp")
    place = lax.axis_index("ctx")
    side = lax.axis_index("tp")
    half_start = side * half
    bf16, f32 = jnp.bfloat16, jnp.float32
    place_word = place.reshape(1).astype(jnp.int32)

    def own_half(value):
        return lax.dynamic_slice_in_dim(value, half_start, half, 0)

    def other_half(value):
        return lax.dynamic_slice_in_dim(value, half - half_start, half, 0)

    rows_in = tokens.reshape(block, width)
    stream = rows_in.astype(f32)
    project_full, output_full = dense_weights(qkv_weight, out_weight)
    first_rows, first_standard, first_spread = norm_input_rows(
        stream, layer_norm_gains[0], layer_norm_biases[0]
    )
    first = first_rows.astype(bf16)
    projected = jnp.einsum(
        "rd,jde->jre", first, project_full, preferred_element_type=f32
    ).astype(bf16)
    far_keys = swap(projected[1, :pslice], "ctx")
    far_values = swap(projected[2, :pslice], "ctx")
    near_out, near_log = run_self_forward(projected)
    context, log_rows = run_cross_forward(
        place_word, projected, far_keys, far_values, near_out, near_log
    )

    route = routes.reshape(half)
    total_experts = experts * owners
    capacity = 2 * half // total_experts
    slots = total_experts * capacity
    group = slots // experts
    member = (route[:, None] == lax.broadcasted_iota(jnp.int32, (half, total_experts), 1)).astype(
        jnp.int32
    )
    rank = jnp.sum((jnp.cumsum(member, axis=0) - 1) * member, axis=1)
    slot_of = (route % experts) * group + (route // experts) * capacity + rank
    placing = (lax.broadcasted_iota(jnp.int32, (slots, half), 0) == slot_of[None, :]).astype(bf16)

    def dispatch(rows):
        spread = jnp.dot(placing, rows, preferred_element_type=f32).astype(bf16)
        spread = spread.reshape(experts, owners, capacity, width)
        return [
            lax.all_to_all(spread[e], "fsdp", split_axis=0, concat_axis=0, tiled=True).reshape(
                group, width
            )
            for e in range(experts)
        ]

    def collect(parts):
        back = [
            lax.all_to_all(
                part.reshape(owners, capacity, width),
                "fsdp",
                split_axis=0,
                concat_axis=0,
                tiled=True,
            ).reshape(group, width)
            for part in parts
        ]
        return jnp.einsum(
            "sr,sd->rd", placing, jnp.concatenate(back, axis=0), preferred_element_type=f32
        )

    upstream_half = own_half(cotangent.reshape(block, width))
    arrived_grad = dispatch(upstream_half)

    sent_half = jnp.dot(other_half(context), output_full, preferred_element_type=f32).astype(bf16)
    kept_half = jnp.dot(own_half(context), output_full, preferred_element_type=f32)
    resid = own_half(rows_in).astype(f32) + kept_half + swap(sent_half, "tp").astype(f32)
    second_rows, second_standard, second_spread = norm_input_rows(
        resid, layer_norm_gains[1], layer_norm_biases[1]
    )
    arrived = dispatch(second_rows.astype(bf16))

    up_full = lax.all_gather(up_weight, ("ctx", "tp"), axis=1, tiled=True)
    down_full = lax.all_gather(down_weight, ("ctx", "tp"), axis=1, tiled=True)
    vectors = lax.all_gather(
        jnp.concatenate([up_shift, down_shift, centroids], axis=1), ("ctx", "tp"), axis=0
    )
    cut = ff // 4
    thin = width // 4

    def whole_vector(start, length):
        return (
            vectors[:, :, start : start + length].transpose(1, 0, 2).reshape(experts, 1, 4 * length)
        )

    up_bias = whole_vector(0, cut)
    down_bias = whole_vector(cut, thin)
    centres = whole_vector(cut + thin, thin)
    there, here = 1 - place, place
    chunk_order = jnp.stack(
        [
            there * 2 + 1 - side,
            here * 2 + 1 - side,
            there * 2 + side,
            here * 2 + side,
        ]
    )
    quarter = jnp.arange(4)
    quarter_place = (quarter % 2 == side) * 2 + (quarter // 2 == place)
    order = jnp.concatenate([chunk_order, quarter_place]).astype(jnp.int32)
    done = [
        run_expert(
            e, order, arrived[e], arrived_grad[e], up_full, down_full, up_bias, down_bias, centres
        )
        for e in range(experts)
    ]

    half_grad = collect([d[1] for d in done]).astype(bf16).astype(f32)
    norm_grad, gain_two, shift_two = norm_back(
        half_grad, second_standard, second_spread, layer_norm_gains[1]
    )
    attended_grad = join_halves((upstream_half.astype(f32) + norm_grad).astype(bf16), side)

    expert_half = collect([d[0] for d in done])
    mixed = join_halves((resid + expert_half).astype(bf16), side)

    up_grad = quarter_sums(
        [d[2].reshape(2, thin, ff) for d in done], [d[3].reshape(2, thin, ff) for d in done]
    )
    down_grad = quarter_sums([d[4] for d in done], [d[5] for d in done])

    def by_quarter(k, length):
        return jnp.stack([d[k].reshape(4, length) for d in done], axis=1)

    small = jnp.concatenate([by_quarter(6, cut), by_quarter(7, thin), by_quarter(8, thin)], axis=2)
    small = small + swap(small, "tp")
    small = small + swap(small, "ctx")
    small = lax.dynamic_index_in_dim(small, place * 2 + side, 0, keepdims=False)
    up_shift_grad = small[:, :cut]
    down_shift_grad = small[:, cut : cut + thin]
    centroids_grad = small[:, cut + thin :]

    output_grad = jnp.einsum("rd,rh->dh", attended_grad, context, preferred_element_type=f32)
    out_grad = scatter_rows(output_grad[None], place)[0].T
    context_grad = jnp.einsum(
        "rd,hd->rh", attended_grad, output_full, preferred_element_type=f32
    ).astype(bf16)
    far_query, far_keys_grad, far_values_grad = run_cross_backward(
        place_word, projected, far_keys, far_values, context_grad, context, log_rows
    )
    keys_back = swap(far_keys_grad, "ctx")
    values_back = swap(far_values_grad, "ctx")
    queries_total, keys_near, values_near = run_self_backward(
        projected, context_grad, context, log_rows, far_query
    )

    def with_far(near, far):
        return jnp.concatenate(
            [near[:pslice] + far.astype(f32), near[pslice:]], axis=0
        ).astype(bf16)

    parts = [queries_total, with_far(keys_near, keys_back), with_far(values_near, values_back)]
    project_grad = jnp.stack(
        [jnp.einsum("rd,re->de", first, part, preferred_element_type=f32) for part in parts]
    )
    qkv_grad = scatter_rows(project_grad, place)
    first_part = sum(
        jnp.einsum("re,de->rd", part, project_full[j], preferred_element_type=f32)
        for j, part in enumerate(parts)
    ).astype(bf16)
    first_grad = first_part.astype(f32) + swap(first_part, "tp").astype(f32)
    stream_grad, gain_one, shift_one = norm_back(
        first_grad, first_standard, first_spread, layer_norm_gains[0]
    )
    tokens_grad = attended_grad.astype(f32) + stream_grad
    two = jnp.stack([gain_two, shift_two])
    two = two + swap(two, "tp")
    norms = jnp.stack([gain_one, two[0], shift_one, two[1]])
    norms = lax.psum_scatter(norms, ("fsdp", "ctx"), scatter_dimension=1, tiled=True)
    return (
        mixed.reshape(1, 1, block, width),
        tokens_grad.reshape(1, 1, block, width),
        qkv_grad,
        out_grad,
        norms[:2],
        norms[2:],
        up_grad,
        up_shift_grad,
        down_grad,
        down_shift_grad,
        centroids_grad,
    )


def solution(mesh):
    paired = mesh.shape["ctx"] == 2 and mesh.shape["tp"] == 2
    in_specs = (
        P("fsdp", "ctx", None, None),
        P("fsdp", "ctx", None, None),
        P("fsdp", "ctx", "tp", None),
        P(None, "fsdp", "tp"),
        P("tp", "fsdp"),
        P(),
        P(),
        P("fsdp", ("ctx", "tp"), None),
        P("fsdp", ("ctx", "tp")),
        P("fsdp", ("ctx", "tp"), None),
        P("fsdp", ("ctx", "tp")),
        P("fsdp", ("ctx", "tp")),
    )
    out_specs = (
        P("fsdp", "ctx", None, None),
        P("fsdp", "ctx", None, None),
        P(None, ("fsdp", "ctx"), "tp"),
        P("tp", ("fsdp", "ctx")),
        P(None, ("fsdp", "ctx")),
        P(None, ("fsdp", "ctx")),
        P("fsdp", ("ctx", "tp"), None),
        P("fsdp", ("ctx", "tp")),
        P("fsdp", ("ctx", "tp"), None),
        P("fsdp", ("ctx", "tp")),
        P("fsdp", ("ctx", "tp")),
    )
    return jax.shard_map(
        shards_pair if paired else shards_any, mesh=mesh, in_specs=in_specs, out_specs=out_specs, check_vma=False)
```

```python
from functools import partial

import jax
import jax.numpy as jnp
from jax import lax
from jax.experimental import pallas as pl
from jax.experimental.pallas import tpu as pltpu
from jax.sharding import PartitionSpec as P

HEAD_DIM = 64
PROMPT = 2048
LEN = 256


EPS = 1e-05
NEG = -1e30


def norm_input_rows(values, gain, shift):
    mean = jnp.mean(values, axis=-1, keepdims=True)
    centred = values - mean
    spread = lax.rsqrt(jnp.mean(centred * centred, axis=-1, keepdims=True) + EPS)
    normed = centred * spread
    return (normed * gain + shift, normed, spread)


def norm_back(upstream, normed, spread, gain):
    scaled = upstream * gain
    inner = (
        scaled
        - jnp.mean(scaled, axis=-1, keepdims=True)
        - normed * jnp.mean(scaled * normed, axis=-1, keepdims=True)
    )
    return (spread * inner, jnp.sum(upstream * normed, axis=0), jnp.sum(upstream, axis=0))


def allowed_keys(place, pslice, prompt, length):
    shape = (pslice + length, prompt + length)
    rows = lax.broadcasted_iota(jnp.int32, shape, 0)
    cols = lax.broadcasted_iota(jnp.int32, shape, 1)
    prompt_row = rows < pslice
    prompt_col = cols < prompt
    early = prompt_row & prompt_col & (cols <= place * pslice + rows)
    later = jnp.logical_not(prompt_row) & (prompt_col | (cols - prompt <= rows - pslice))
    return early | later


def dense_weights(qkv_weight, out_weight):
    return (
        lax.all_gather(qkv_weight, "fsdp", axis=1, tiled=True),
        lax.all_gather(out_weight, "fsdp", axis=1, tiled=True),
    )


def expert_weights(up_weight, down_weight, up_shift, down_shift, centroids):
    return (
        lax.all_gather(up_weight, ("ctx", "tp"), axis=1, tiled=True),
        lax.all_gather(down_weight, ("ctx", "tp"), axis=1, tiled=True),
        lax.all_gather(up_shift, ("ctx", "tp"), axis=1, tiled=True),
        lax.all_gather(down_shift, ("ctx", "tp"), axis=1, tiled=True),
        lax.all_gather(centroids, ("ctx", "tp"), axis=1, tiled=True),
    )


def tp_rows(rows):
    return lax.all_gather(rows, "tp", axis=0, tiled=True)


def head_total(terms):
    return lax.psum(terms.astype(jnp.bfloat16), "tp").astype(jnp.float32)


def split_heads(matrix):
    return matrix.reshape(matrix.shape[0], -1, HEAD_DIM).transpose(1, 0, 2)


def join_heads(stacked):
    return stacked.transpose(1, 0, 2).reshape(stacked.shape[1], -1)


def head_forward(allowed, scale, parts):
    query, keys, values = parts
    raw = jnp.einsum("qd,kd->qk", query, keys, preferred_element_type=jnp.float32) * scale
    scores = jnp.where(allowed, raw, NEG)
    top = jnp.max(scores, axis=-1, keepdims=True)
    weights = jnp.exp(scores - top)
    total = jnp.sum(weights, axis=-1, keepdims=True)
    shares = (weights / total).astype(jnp.bfloat16)
    context = jnp.dot(shares, values, preferred_element_type=jnp.float32).astype(jnp.bfloat16)
    return (context, (top + jnp.log(total))[:, 0])


def head_backward(allowed, scale, parts):
    query, keys, values, context_grad, log_total = parts
    raw = jnp.einsum("qd,kd->qk", query, keys, preferred_element_type=jnp.float32) * scale
    scores = jnp.where(allowed, raw, NEG)
    weights = jnp.exp(scores - log_total[:, None])
    values_grad = jnp.einsum(
        "qk,qd->kd", weights.astype(jnp.bfloat16), context_grad, preferred_element_type=jnp.float32
    )
    weight_grad = jnp.einsum("qd,kd->qk", context_grad, values, preferred_element_type=jnp.float32)
    row_dot = jnp.sum(weights * weight_grad, axis=-1, keepdims=True)
    logit_grad = (weights * (weight_grad - row_dot)).astype(jnp.bfloat16)
    query_grad = jnp.dot(logit_grad, keys, preferred_element_type=jnp.float32) * scale
    keys_grad = (
        jnp.einsum("qk,qd->kd", logit_grad, query, preferred_element_type=jnp.float32) * scale
    )
    return (query_grad, keys_grad, values_grad)


def shards_any(
    tokens,
    cotangent,
    routes,
    qkv_weight,
    out_weight,
    layer_norm_gains,
    layer_norm_biases,
    up_weight,
    up_shift,
    down_weight,
    down_shift,
    centroids,
):
    block = tokens.shape[2]
    width = tokens.shape[3]
    pslice = block - LEN
    half = routes.shape[2]
    place = lax.axis_index("ctx")
    half_start = lax.axis_index("tp") * half
    scale = HEAD_DIM ** (-0.5)
    residual_stream = tokens.reshape(block, width).astype(jnp.float32)
    project_full, output_full = dense_weights(qkv_weight, out_weight)
    first_normed_rows, first_standardized, first_deviation = norm_input_rows(
        residual_stream, layer_norm_gains[0], layer_norm_biases[0]
    )
    first = first_normed_rows.astype(jnp.bfloat16)
    projected = jnp.einsum(
        "rd,jde->jre", first, project_full, preferred_element_type=jnp.float32
    ).astype(jnp.bfloat16)
    queries, keys_own, values_own = (projected[0], projected[1], projected[2])
    prompt_keys, prompt_values = (
        lax.all_gather(keys_own[:pslice], "ctx", axis=0, tiled=True),
        lax.all_gather(values_own[:pslice], "ctx", axis=0, tiled=True),
    )
    keys_all = jnp.concatenate([prompt_keys, keys_own[pslice:]], axis=0)
    values_all = jnp.concatenate([prompt_values, values_own[pslice:]], axis=0)
    allowed = allowed_keys(place, pslice, PROMPT, LEN)
    query_heads = split_heads(queries)
    key_heads = split_heads(keys_all)
    value_heads = split_heads(values_all)
    context_heads, log_total = lax.map(
        partial(head_forward, allowed, scale), (query_heads, key_heads, value_heads)
    )
    context = join_heads(context_heads)
    attended = head_total(jnp.dot(context, output_full, preferred_element_type=jnp.float32))
    residual_rows = residual_stream + attended
    second_normed_rows, second_standardized, second_deviation = norm_input_rows(
        residual_rows, layer_norm_gains[1], layer_norm_biases[1]
    )
    second = second_normed_rows.astype(jnp.bfloat16)
    own_rows = lax.dynamic_slice_in_dim(second, half_start, half, 0)
    route = routes.reshape(half)
    local_experts = up_weight.shape[0]
    owners = lax.axis_size("fsdp")
    total_experts = local_experts * owners
    capacity = 2 * half // total_experts
    slots = total_experts * capacity
    member = (route[:, None] == lax.broadcasted_iota(jnp.int32, (half, total_experts), 1)).astype(
        jnp.int32
    )
    rank = jnp.sum((jnp.cumsum(member, axis=0) - 1) * member, axis=1)
    slot_of = route * capacity + rank
    placing = (lax.broadcasted_iota(jnp.int32, (slots, half), 0) == slot_of[None, :]).astype(
        jnp.bfloat16
    )
    outgoing = (
        jnp.dot(placing, own_rows, preferred_element_type=jnp.float32)
        .astype(jnp.bfloat16)
        .reshape(owners, local_experts, capacity, width)
    )
    up_full, down_full, up_bias, down_bias, centres = expert_weights(
        up_weight, down_weight, up_shift, down_shift, centroids
    )
    arrived = lax.all_to_all(outgoing, "fsdp", split_axis=0, concat_axis=0, tiled=True)
    score = jnp.einsum("sekd,ed->sek", arrived, centres, preferred_element_type=jnp.float32)
    gate = jax.nn.sigmoid(score)
    inner = jnp.einsum(
        "sekd,edf->sekf", arrived, up_full, preferred_element_type=jnp.float32
    ) + up_bias[None, :, None, :].astype(jnp.float32)
    hidden = jax.nn.gelu(inner, approximate=False).astype(jnp.bfloat16)
    result = jnp.einsum(
        "sekf,efd->sekd", hidden, down_full, preferred_element_type=jnp.float32
    ) + down_bias[None, :, None, :].astype(jnp.float32)
    sent = (gate[..., None] * result).astype(jnp.bfloat16)
    returned = lax.all_to_all(sent, "fsdp", split_axis=0, concat_axis=0, tiled=True)
    returned, arrived, inner, hidden, gate, result = (
        returned,
        arrived,
        inner,
        hidden,
        gate,
        result,
    )
    back_rows = jnp.einsum(
        "sr,sd->rd", placing, returned.reshape(slots, width), preferred_element_type=jnp.float32
    ).astype(jnp.bfloat16)
    expert_out = tp_rows(back_rows)
    mixed = (residual_rows + expert_out.astype(jnp.float32)).astype(jnp.bfloat16)
    project_back, output_back = dense_weights(qkv_weight, out_weight)
    up_back, down_back, unused_up, unused_down, centre_back = expert_weights(
        up_weight, down_weight, up_shift, down_shift, centroids
    )
    upstream_rows = cotangent.reshape(block, width)
    upstream = upstream_rows.astype(jnp.float32)
    upstream_half = lax.dynamic_slice_in_dim(upstream_rows, half_start, half, 0)
    grad_out = (
        jnp.dot(placing, upstream_half, preferred_element_type=jnp.float32)
        .astype(jnp.bfloat16)
        .reshape(owners, local_experts, capacity, width)
    )
    arrived_grad = lax.all_to_all(grad_out, "fsdp", split_axis=0, concat_axis=0, tiled=True).astype(
        jnp.float32
    )
    result_grad = (gate[..., None] * arrived_grad).astype(jnp.bfloat16)
    gate_grad = jnp.sum(arrived_grad * result, axis=-1)
    score_grad = (gate_grad * gate * (1.0 - gate)).astype(jnp.bfloat16)
    hidden_grad = jnp.einsum(
        "sekd,efd->sekf", result_grad, down_back, preferred_element_type=jnp.float32
    )
    gelu_pull = jax.vjp(partial(jax.nn.gelu, approximate=False), inner)[1]
    inner_grad = gelu_pull(hidden_grad)[0].astype(jnp.bfloat16)
    rows_grad = jnp.einsum(
        "sekf,edf->sekd", inner_grad, up_back, preferred_element_type=jnp.float32
    )
    rows_grad = rows_grad + score_grad.astype(jnp.float32)[..., None] * centre_back[
        None, :, None, :
    ].astype(jnp.float32)
    sent_grad = lax.all_to_all(
        rows_grad.astype(jnp.bfloat16), "fsdp", split_axis=0, concat_axis=0, tiled=True
    )
    up_local = jnp.einsum("sekd,sekf->edf", arrived, inner_grad, preferred_element_type=jnp.float32)
    down_local = jnp.einsum(
        "sekf,sekd->efd", hidden, result_grad, preferred_element_type=jnp.float32
    )
    up_shift_local = jnp.sum(inner_grad.astype(jnp.float32), axis=(0, 2))
    down_shift_local = jnp.sum(result_grad.astype(jnp.float32), axis=(0, 2))
    centre_local = jnp.einsum(
        "sek,sekd->ed", score_grad, arrived, preferred_element_type=jnp.float32
    )
    up_grad, down_grad, up_shift_grad, down_shift_grad, centroids_grad = (
        lax.psum_scatter(
            up_local.astype(jnp.bfloat16), ("ctx", "tp"), scatter_dimension=1, tiled=True
        ).astype(jnp.float32),
        lax.psum_scatter(
            down_local.astype(jnp.bfloat16), ("ctx", "tp"), scatter_dimension=1, tiled=True
        ).astype(jnp.float32),
        lax.psum_scatter(
            up_shift_local.astype(jnp.bfloat16), ("ctx", "tp"), scatter_dimension=1, tiled=True
        ).astype(jnp.float32),
        lax.psum_scatter(
            down_shift_local.astype(jnp.bfloat16), ("ctx", "tp"), scatter_dimension=1, tiled=True
        ).astype(jnp.float32),
        lax.psum_scatter(
            centre_local.astype(jnp.bfloat16), ("ctx", "tp"), scatter_dimension=1, tiled=True
        ).astype(jnp.float32),
    )
    half_grad = jnp.einsum(
        "sr,sd->rd", placing, sent_grad.reshape(slots, width), preferred_element_type=jnp.float32
    ).astype(jnp.bfloat16)
    second_norm_gradient = tp_rows(half_grad).astype(jnp.float32)
    resid_norm_grad, gain_two_grad, shift_two_grad = norm_back(
        second_norm_gradient, second_standardized, second_deviation, layer_norm_gains[1]
    )
    resid_grad = upstream + resid_norm_grad
    attended_grad = resid_grad.astype(jnp.bfloat16)
    output_grad = jnp.einsum(
        "rh,rd->hd", context, attended_grad, preferred_element_type=jnp.float32
    )
    context_grad = jnp.einsum(
        "rd,hd->rh", attended_grad, output_back, preferred_element_type=jnp.float32
    ).astype(jnp.bfloat16)
    query_grad, keys_grad, values_grad = lax.map(
        partial(head_backward, allowed, scale),
        (query_heads, key_heads, value_heads, split_heads(context_grad), log_total),
    )
    keys_flat = join_heads(keys_grad)
    values_flat = join_heads(values_grad)
    prompt_key_grad, prompt_value_grad = (
        lax.psum_scatter(
            keys_flat[:PROMPT].astype(jnp.bfloat16), "ctx", scatter_dimension=0, tiled=True
        ).astype(jnp.float32),
        lax.psum_scatter(
            values_flat[:PROMPT].astype(jnp.bfloat16), "ctx", scatter_dimension=0, tiled=True
        ).astype(jnp.float32),
    )
    keys_total = jnp.concatenate([prompt_key_grad, keys_flat[PROMPT:]], axis=0).astype(jnp.bfloat16)
    values_total = jnp.concatenate([prompt_value_grad, values_flat[PROMPT:]], axis=0).astype(
        jnp.bfloat16
    )
    queries_total = join_heads(query_grad).astype(jnp.bfloat16)
    stacked = jnp.stack([queries_total, keys_total, values_total])
    project_grad = jnp.einsum("rd,jre->jde", first, stacked, preferred_element_type=jnp.float32)
    first_norm_gradient = head_total(
        jnp.einsum("jre,jde->rd", stacked, project_back, preferred_element_type=jnp.float32)
    )
    stream_norm_grad, gain_one_grad, shift_one_grad = norm_back(
        first_norm_gradient, first_standardized, first_deviation, layer_norm_gains[0]
    )
    tokens_grad = resid_grad + stream_norm_grad
    gains_local = jnp.stack([gain_one_grad, gain_two_grad])
    shifts_local = jnp.stack([shift_one_grad, shift_two_grad])
    qkv_grad, out_grad, gains_grad, shifts_grad = (
        lax.psum_scatter(project_grad, ("fsdp", "ctx"), scatter_dimension=1, tiled=True),
        lax.psum_scatter(output_grad, ("fsdp", "ctx"), scatter_dimension=1, tiled=True),
        lax.psum_scatter(gains_local, ("fsdp", "ctx"), scatter_dimension=1, tiled=True),
        lax.psum_scatter(shifts_local, ("fsdp", "ctx"), scatter_dimension=1, tiled=True),
    )
    return (
        mixed.reshape(1, 1, block, width),
        tokens_grad.reshape(1, 1, block, width),
        qkv_grad,
        out_grad,
        gains_grad,
        shifts_grad,
        up_grad,
        up_shift_grad,
        down_grad,
        down_shift_grad,
        centroids_grad,
    )


F32 = jnp.float32
BF = jnp.bfloat16
NT = (((1,), (1,)), ((), ()))
TN = (((0,), (0,)), ((), ()))
TILE = 256
PAIR = 2 * HEAD_DIM


def nt(a, b):
    return lax.dot_general(a, b, NT, preferred_element_type=F32)


def tn(a, b):
    return lax.dot_general(a, b, TN, preferred_element_type=F32)


def mm(a, b):
    return jnp.dot(a, b, preferred_element_type=F32)


def head_masks(rows):
    lane = lax.broadcasted_iota(jnp.int32, (rows, PAIR), 1)
    return (lane < HEAD_DIM, lane >= HEAD_DIM)


def self_forward(q_ref, k_ref, v_ref, o_ref, lse_ref):
    rows = q_ref.shape[0]
    lo, hi = head_masks(TILE)
    tri = lax.broadcasted_iota(jnp.int32, (TILE, TILE), 1) <= lax.broadcasted_iota(
        jnp.int32, (TILE, TILE), 0
    )
    for i in range(rows // TILE):
        at = pl.ds(i * TILE, TILE)
        q = q_ref[at, :] * jnp.asarray(HEAD_DIM**-0.5, BF)
        outs, lses = [], []
        for mask in (lo, hi):
            qm = jnp.where(mask, q, jnp.zeros_like(q))
            diag = jnp.where(tri, nt(qm, k_ref[at, :]), NEG)
            top = jnp.max(diag, axis=1, keepdims=True)
            if i:
                off = nt(qm, k_ref[: i * TILE, :])
                top = jnp.maximum(top, jnp.max(off, axis=1, keepdims=True))
            near = jnp.exp(diag - top)
            total = jnp.sum(near, axis=1, keepdims=True)
            acc = mm(near.astype(BF), v_ref[at, :])
            if i:
                early = jnp.exp(off - top)
                total = total + jnp.sum(early, axis=1, keepdims=True)
                acc = acc + mm(early.astype(BF), v_ref[: i * TILE, :])
            outs.append(acc / total)
            lses.append(top + jnp.log(total))
        o_ref[at, :] = jnp.where(lo, outs[0], outs[1])
        lse_ref[at, :] = jnp.where(lo, lses[0], lses[1])


def cross_forward(word_ref, q_ref, k_ref, v_ref, o_ref, lse_ref, *rest):
    ctx_ref, log_ref = rest[-2:]
    rows = q_ref.shape[0]
    lo, hi = head_masks(TILE)

    def put(i, o, lse):
        at = pl.ds(i * TILE, TILE)
        ctx_ref[at, :] = o.astype(BF)
        flipped = lse.T
        log_ref[0:1, at] = flipped[0:1, :]
        log_ref[1:2, at] = flipped[HEAD_DIM : HEAD_DIM + 1, :]

    def tile(i):
        at = pl.ds(i * TILE, TILE)
        q = q_ref[at, :] * jnp.asarray(HEAD_DIM**-0.5, BF)
        outs, lses = [], []
        for mask in (lo, hi):
            s = nt(jnp.where(mask, q, jnp.zeros_like(q)), k_ref[...])
            top = jnp.max(s, axis=1, keepdims=True)
            p = jnp.exp(s - top)
            total = jnp.sum(p, axis=1, keepdims=True)
            outs.append(mm(p.astype(BF), v_ref[...]) / total)
            lses.append(top + jnp.log(total))
        o_far = jnp.where(lo, outs[0], outs[1])
        l_far = jnp.where(lo, lses[0], lses[1])
        l_near = lse_ref[at, :]
        top = jnp.maximum(l_near, l_far)
        near, far = jnp.exp(l_near - top), jnp.exp(l_far - top)
        both = near + far
        put(i, (o_ref[at, :] * near + o_far * far) / both, top + jnp.log(both))

    def keep(i):
        at = pl.ds(i * TILE, TILE)
        put(i, o_ref[at, :], lse_ref[at, :])

    later = word_ref[0] == 1
    for i in range(rows // TILE):
        if i >= k_ref.shape[0] // TILE:
            tile(i)
        else:
            pl.when(later)(partial(tile, i))
            pl.when(jnp.logical_not(later))(partial(keep, i))


def row_dots(g, o):
    prod = (g.astype(F32) * o.astype(F32)).T
    return (
        jnp.sum(prod[:HEAD_DIM], axis=0, keepdims=True),
        jnp.sum(prod[HEAD_DIM:], axis=0, keepdims=True),
    )


def pair_back(q, g, k, v, kt, lse, dots, masks, visible):
    ps, ds, qs, gs, dq = [], [], [], [], []
    for h in range(2):
        qm = jnp.where(masks[h], q, jnp.zeros_like(q))
        gm = jnp.where(masks[h], g, jnp.zeros_like(g))
        p = jnp.exp(nt(k, qm) - lse[h])
        if visible is not None:
            p = jnp.where(visible, p, 0.0)
        d = (p * (nt(v, gm) - dots[h])).astype(BF)
        ps.append(p.astype(BF))
        ds.append(d)
        qs.append(qm)
        gs.append(gm)
        dq.append(mm(kt[h * HEAD_DIM : (h + 1) * HEAD_DIM, :], d))
    dv = mm(jnp.concatenate(ps, axis=1), jnp.concatenate(gs, axis=0))
    dk = mm(jnp.concatenate(ds, axis=1), jnp.concatenate(qs, axis=0))
    return jnp.concatenate(dq, axis=0), dk, dv


def cross_backward(word_ref, q_ref, k_ref, v_ref, g_ref, c_ref, log_ref, dq_ref, dkv_ref, dk_acc, dv_acc):
    rows, keys = q_ref.shape[0], k_ref.shape[0]
    masks = head_masks(TILE)
    dk_acc[...] = jnp.zeros_like(dk_acc)
    dv_acc[...] = jnp.zeros_like(dv_acc)
    kt = k_ref[...].T

    def tile(i):
        at = pl.ds(i * TILE, TILE)
        q = q_ref[at, :] * jnp.asarray(HEAD_DIM**-0.5, BF)
        g = g_ref[at, :]
        dots = row_dots(g, c_ref[at, :])
        lse = (log_ref[0:1, at], log_ref[1:2, at])
        dq, dk, dv = pair_back(q, g, k_ref[...], v_ref[...], kt, lse, dots, masks, None)
        dq_ref[:, at] = dq
        dk_acc[...] += dk
        dv_acc[...] += dv

    def skip(i):
        dq_ref[:, pl.ds(i * TILE, TILE)] = jnp.zeros((PAIR, TILE), F32)

    later = word_ref[0] == 1
    for i in range(rows // TILE):
        if i >= keys // TILE:
            tile(i)
        else:
            pl.when(later)(partial(tile, i))
            pl.when(jnp.logical_not(later))(partial(skip, i))
    dkv_ref[:, :PAIR] = dk_acc[...].astype(BF)
    dkv_ref[:, PAIR:] = dv_acc[...].astype(BF)


def self_backward(q_ref, k_ref, v_ref, g_ref, c_ref, log_ref, dqx_ref, far_ref, *rest):
    out_ref, dk_acc, dv_acc = rest[-3:]
    rows, keys = q_ref.shape[0], far_ref.shape[0]
    masks = head_masks(TILE)
    dk_acc[:keys, :] = far_ref[:, :PAIR].astype(F32)
    dv_acc[:keys, :] = far_ref[:, PAIR:].astype(F32)
    dk_acc[keys:, :] = jnp.zeros((rows - keys, PAIR), F32)
    dv_acc[keys:, :] = jnp.zeros((rows - keys, PAIR), F32)
    kt = k_ref[...].T
    seen = lax.broadcasted_iota(jnp.int32, (TILE, TILE), 0) <= lax.broadcasted_iota(
        jnp.int32, (TILE, TILE), 1
    )
    for i in range(rows // TILE):
        at = pl.ds(i * TILE, TILE)
        q = q_ref[at, :] * jnp.asarray(HEAD_DIM**-0.5, BF)
        g = g_ref[at, :]
        dots = row_dots(g, c_ref[at, :])
        lse = (log_ref[0:1, at], log_ref[1:2, at])
        dq, dk, dv = pair_back(
            q, g, k_ref[at, :], v_ref[at, :], kt[:, i * TILE : (i + 1) * TILE], lse, dots, masks, seen
        )
        dk_acc[at, :] += dk
        dv_acc[at, :] += dv
        if i:
            n = i * TILE
            dq_early, dk, dv = pair_back(
                q, g, k_ref[:n, :], v_ref[:n, :], kt[:, :n], lse, dots, masks, None
            )
            dq = dq + dq_early
            dk_acc[:n, :] += dk
            dv_acc[:n, :] += dv
        out_ref[at, :PAIR] = ((dq + dqx_ref[:, at]) * (HEAD_DIM**-0.5)).T.astype(BF)
    out_ref[:, PAIR : 2 * PAIR] = dk_acc[...].astype(BF)
    out_ref[:, 2 * PAIR :] = dv_acc[...].astype(BF)


def column(rows, width, at):
    return pl.BlockSpec((rows, width), lambda *_: (0, at))


ANY = pl.BlockSpec(memory_space=pl.ANY)


def shape(dims, dtype):
    return jax.ShapeDtypeStruct(dims, dtype)


def cost(elements, matmuls):
    return pl.CostEstimate(
        flops=2 * elements * PAIR * matmuls, transcendentals=elements, bytes_accessed=4 * 1280 * 1024
    )


def run_self_forward(qkv, width):
    rows = qkv.shape[0]
    spec = lambda j: pl.BlockSpec((rows, PAIR), lambda p: (0, 3 * p + j))
    out = pl.BlockSpec((rows, PAIR), lambda p: (0, p))
    return pl.pallas_call(
        self_forward,
        grid=(width // PAIR,),
        in_specs=[spec(0), spec(1), spec(2)],
        out_specs=[out, out],
        out_shape=[shape((rows, width), F32)] * 2,
        cost_estimate=cost(6 * rows * rows, 4),
        name="self_forward",
    )(qkv, qkv, qkv)


def run_cross_forward(p, word, qkv, far, out, lse, carried):
    rows, width = out.shape
    keys = far.shape[0]
    return pl.pallas_call(
        cross_forward,
        grid_spec=pltpu.PrefetchScalarGridSpec(
            num_scalar_prefetch=1,
            grid=(1,),
            in_specs=[
                column(rows, PAIR, 3 * p),
                column(keys, PAIR, 0),
                column(keys, PAIR, 1),
                column(rows, PAIR, p),
                column(rows, PAIR, p),
            ]
            + [ANY] * len(carried),
            out_specs=[
                column(rows, PAIR, p),
                pl.BlockSpec((None, 2, rows), lambda *_: (p, 0, 0)),
            ],
        ),
        out_shape=[shape((rows, width), BF), shape((width // PAIR, 2, rows), F32)],
        input_output_aliases={6 + i: i for i in range(len(carried))},
        cost_estimate=cost(2 * rows * keys, 4),
        name=f"cross_forward_{p}",
    )(word, qkv, far, far, out, lse, *carried)


def run_cross_backward(p, word, qkv, far, g, context, log_rows):
    rows = g.shape[0]
    keys = far.shape[0]
    return pl.pallas_call(
        cross_backward,
        grid_spec=pltpu.PrefetchScalarGridSpec(
            num_scalar_prefetch=1,
            grid=(1,),
            in_specs=[
                column(rows, PAIR, 3 * p),
                column(keys, PAIR, 0),
                column(keys, PAIR, 1),
                column(rows, PAIR, p),
                column(rows, PAIR, p),
                pl.BlockSpec((None, 2, rows), lambda *_: (p, 0, 0)),
            ],
            out_specs=[column(PAIR, rows, 0), column(keys, 2 * PAIR, 0)],
            scratch_shapes=[pltpu.VMEM((keys, PAIR), F32)] * 2,
        ),
        out_shape=[shape((PAIR, rows), F32), shape((keys, 2 * PAIR), BF)],
        cost_estimate=cost(2 * rows * keys, 8),
        name=f"cross_backward_{p}",
    )(word, qkv, far, far, g, context, log_rows)


def run_self_backward(p, qkv, g, context, log_rows, far_query, far, carried):
    rows, width = g.shape
    keys = far.shape[0]
    return pl.pallas_call(
        self_backward,
        grid=(1,),
        in_specs=[
            column(rows, PAIR, 3 * p),
            column(rows, PAIR, 3 * p + 1),
            column(rows, PAIR, 3 * p + 2),
            column(rows, PAIR, p),
            column(rows, PAIR, p),
            pl.BlockSpec((None, 2, rows), lambda *_: (p, 0, 0)),
            column(PAIR, rows, 0),
            column(keys, 2 * PAIR, 0),
        ]
        + [ANY] * len(carried),
        out_specs=column(rows, 3 * PAIR, p),
        out_shape=shape((rows, 3 * width), BF),
        scratch_shapes=[pltpu.VMEM((rows, PAIR), F32)] * 2,
        input_output_aliases={8: 0} if carried else {},
        cost_estimate=cost(rows * rows, 8),
        name=f"self_backward_{p}",
    )(qkv, qkv, qkv, g, context, log_rows, far_query, far, *carried)


ROOT_HALF = 0.7071067811865476
DENSITY = 0.3989422804014327


def quarter_of(j, word):
    return 2 * (word[0] ^ 1 ^ (j & 1)) + (word[1] ^ 1 ^ (j >> 1))


def expert_step(index, word_ref, x_ref, cot_ref, *refs):
    ups, downs, vec_ref = refs[:4], refs[4:8], refs[8]
    carried = 2 * index
    sent_ref, small_ref, dx_ref, gu_ref, ku_ref, gd_ref, kd_ref = refs[9 + carried : 16 + carried]
    rg, xt, gate, res, dx, up, down = refs[16 + carried :]
    small_in = refs[10] if index else None
    j = pl.program_id(0)
    rows, width = x_ref.shape
    thin = width // 4
    cut = down.shape[0]
    ff = 4 * cut
    bias_at = pl.ds(pl.multiple_of(quarter_of(j, word_ref) * cut, cut), cut)
    down_bias = vec_ref[0:1, ff : ff + width].astype(F32)
    centre = vec_ref[0:1, ff + width :].astype(F32)

    @pl.when(j == 0)
    def _():
        x = x_ref[...]
        score = jnp.sum(x.astype(F32) * centre, axis=1, keepdims=True)
        g = jax.nn.sigmoid(score)
        gate[...] = jnp.broadcast_to(g, gate.shape)
        r = (g * cot_ref[...].reshape(rows, width).astype(F32)).astype(BF)
        rg[...] = r
        small_ref[...] = small_in[...] if index else jnp.zeros_like(small_ref)
        small_ref[2:3, index * width : (index + 1) * width] = jnp.sum(
            r.astype(F32), axis=0, keepdims=True
        )
        t = x.T
        for s in range(4):
            at = 2 * (1 ^ word_ref[1] ^ (s & 1)) + (1 ^ word_ref[0] ^ (s >> 1))
            xt[pl.ds(pl.multiple_of(at * thin, thin), thin), :] = t[s * thin : (s + 1) * thin, :]
        res[...] = jnp.zeros_like(res)
        dx[...] = jnp.zeros_like(dx)

    for k in range(4):
        at = quarter_of(k, word_ref)
        up[pl.ds(pl.multiple_of(at * thin, thin), thin), :] = ups[k][...]

        @pl.when(j == k)
        def _():
            down[...] = downs[k][...]

    r = rg[...]
    inner = mm(x_ref[...], up[...]) + vec_ref[0:1, bias_at].astype(F32)
    cdf = 0.5 * (1.0 + lax.erf(inner * ROOT_HALF))
    hidden = (inner * cdf).astype(BF)
    slope = cdf + inner * (jnp.exp(-0.5 * inner * inner) * DENSITY)
    res[...] += mm(hidden, down[...])
    back = (nt(r, down[...]) * slope).astype(BF)
    small_ref[index : index + 1, bias_at] = jnp.sum(back.astype(F32), axis=0, keepdims=True)
    dx[...] += nt(back, up[...])
    grad = mm(xt[...], back)
    gu_ref[...] = grad[: 2 * thin].astype(BF)
    ku_ref[...] = grad[2 * thin :].astype(BF)
    grad = tn(hidden, r).astype(BF)

    @pl.when(j < 2)
    def _():
        gd_ref[...] = grad

    @pl.when(j >= 2)
    def _():
        kd_ref[...] = grad

    @pl.when(j == 3)
    def _():
        g = gate[:, :1]
        out = res[...] + down_bias
        sent_ref[...] = (g * out).astype(BF).reshape(sent_ref.shape)
        cot = cot_ref[...].reshape(rows, width).astype(F32)
        sg = jnp.sum(cot * out, axis=1, keepdims=True) * g * (1.0 - g)
        sg = sg.astype(BF).astype(F32)
        dx_ref[...] = (dx[...] + sg * centre).astype(BF)
        small_ref[2:3, (2 + index) * width : (3 + index) * width] = jnp.sum(
            sg * x_ref[...].astype(F32), axis=0, keepdims=True
        )


def run_expert(index, word, x, cot, ups, downs, vectors, carried):
    rows, width = x.shape
    owners, experts, capacity, _ = cot.shape
    ff = ups[0].shape[2]
    cut, thin = ff // 4, width // 4
    whole = lambda *dims: pl.BlockSpec(dims, lambda j, w: (0,) * len(dims))
    slot = pl.BlockSpec((owners, None, capacity, width), lambda j, w: (0, index, 0, 0))
    upper = pl.BlockSpec((2, thin, cut), lambda j, w: (0, 0, quarter_of(j, w)))
    half_up = pl.BlockSpec((2 * thin, cut), lambda j, w: (0, quarter_of(j, w)))
    assert experts == 2
    return pl.pallas_call(
        partial(expert_step, index),
        grid_spec=pltpu.PrefetchScalarGridSpec(
            num_scalar_prefetch=1,
            grid=(4,),
            in_specs=[whole(rows, width), slot]
            + [pl.BlockSpec((None, thin, cut), lambda j, w: (index, 0, quarter_of(j, w)))] * 4
            + [pl.BlockSpec((None, cut, width), lambda j, w: (index, 0, 0))] * 4
            + [pl.BlockSpec((None, 1, ff + 2 * width), lambda j, w: (index, 0, 0))]
            + ([ANY, whole(8, ff)] if carried else []),
            out_specs=[
                slot,
                whole(8, ff),
                whole(rows, width),
                half_up,
                half_up,
                pl.BlockSpec((None, cut, width), lambda j, w: (jnp.minimum(j, 1), 0, 0)),
                pl.BlockSpec((None, cut, width), lambda j, w: (jnp.maximum(j, 2) - 2, 0, 0)),
            ],
            scratch_shapes=[
                pltpu.VMEM((rows, width), BF),
                pltpu.VMEM((width, rows), BF),
                pltpu.VMEM((rows, 128), F32),
                pltpu.VMEM((rows, width), F32),
                pltpu.VMEM((rows, width), F32),
                pltpu.VMEM((width, cut), BF),
                pltpu.VMEM((cut, width), BF),
            ],
        ),
        out_shape=[
            shape(cot.shape, BF),
            shape((8, ff), F32),
            shape((rows, width), BF),
            shape((2 * thin, ff), BF),
            shape((2 * thin, ff), BF),
            shape((2, cut, width), BF),
            shape((2, cut, width), BF),
        ],
        input_output_aliases={12: 0} if carried else {},
        cost_estimate=pl.CostEstimate(
            flops=12 * rows * width * ff, transcendentals=2 * rows * ff, bytes_accessed=24 << 20
        ),
        name=f"expert_{index}",
    )(word, x, cot, *ups, *downs, vectors, *carried)


SWAP = ((0, 1), (1, 0))


def swap(value, axis):
    return lax.ppermute(value, axis, SWAP)


def after(value, *others):
    return lax.optimization_barrier((value,) + others)[0]


def spread_rows(value, axis=0):
    return lax.all_to_all(value, "fsdp", split_axis=axis, concat_axis=axis, tiled=True)


def scope(name):
    return jax.named_scope(name)


def shards_pair(
    tokens,
    cotangent,
    routes,
    qkv_weight,
    out_weight,
    layer_norm_gains,
    layer_norm_biases,
    up_weight,
    up_shift,
    down_weight,
    down_shift,
    centroids,
):
    block, width = tokens.shape[2:]
    pslice = block - LEN
    half = routes.shape[2]
    experts, thin, ff = up_weight.shape
    cut = down_weight.shape[1]
    owners = lax.axis_size("fsdp")
    place = lax.axis_index("ctx")
    side = lax.axis_index("tp")
    half_start = side * half
    word = jnp.stack([place, side]).astype(jnp.int32)
    local = qkv_weight.shape[2]
    pairs = local // PAIR

    def own_half(value):
        return lax.dynamic_slice_in_dim(value, half_start, half, 0)

    def other_half(value):
        return lax.dynamic_slice_in_dim(value, half - half_start, half, 0)

    def join_halves(own):
        other = swap(own, "tp")
        buffer = jnp.zeros((block, width), own.dtype)
        buffer = lax.dynamic_update_slice_in_dim(buffer, own, half_start, 0)
        return lax.dynamic_update_slice_in_dim(buffer, other, half - half_start, 0)

    packed = qkv_weight.reshape(3, -1, pairs, PAIR).transpose(1, 2, 0, 3).reshape(-1, 3 * local)
    with scope("gather_qkv"):
        project = lax.all_gather(packed, "fsdp", axis=0, tiled=True)
    with scope("gather_out"):
        output = lax.all_gather(out_weight.T, "fsdp", axis=0, tiled=True)
    with scope("up_ctx"):
        up_far = swap(up_weight, "ctx")

    rows_in = tokens.reshape(block, width)
    first_rows, first_standard, first_spread = norm_input_rows(
        rows_in.astype(F32), layer_norm_gains[0], layer_norm_biases[0]
    )
    first = first_rows.astype(BF)
    projected = jnp.dot(first, project, preferred_element_type=F32).astype(BF)
    far = []
    for p in range(pairs):
        start = (3 * p + 1) * PAIR
        with scope(f"far_{p}"):
            far.append(swap(projected[:pslice, start : start + 2 * PAIR], "ctx"))

    with scope("down_ctx"):
        down_far = swap(after(down_weight, far[0]), "ctx")
    vector = jnp.concatenate([up_shift, down_shift, centroids], axis=1)
    vector_far = swap(vector, "ctx")
    with scope("up_tp"):
        up_side, up_both = swap(up_weight, "tp"), swap(up_far, "tp")
    with scope("down_tp"):
        down_side, down_both = swap(down_weight, "tp"), swap(down_far, "tp")
    vector_side, vector_both = swap(vector, "tp"), swap(vector_far, "tp")
    ups = (up_both, up_side, up_far, up_weight)
    downs = (down_both, down_side, down_far, down_weight)
    by_quarter = [
        jnp.where(
            side == s % 2,
            jnp.where(place == s // 2, vector, vector_far),
            jnp.where(place == s // 2, vector_side, vector_both),
        )
        for s in range(4)
    ]
    vectors = jnp.concatenate(
        [v[:, :cut] for v in by_quarter]
        + [v[:, cut : cut + thin] for v in by_quarter]
        + [v[:, cut + thin :] for v in by_quarter],
        axis=1,
    )[:, None]

    route = routes.reshape(half)
    total_experts = experts * owners
    capacity = 2 * half // total_experts
    member = (route[:, None] == lax.broadcasted_iota(jnp.int32, (half, total_experts), 1)).astype(
        jnp.int32
    )
    rank = jnp.sum((jnp.cumsum(member, axis=0) - 1) * member, axis=1)
    slot_of = (route // experts) * capacity + rank
    slots = lax.broadcasted_iota(jnp.int32, (owners * capacity, half), 0)
    placing = [
        ((slots == slot_of[None, :]) & (route % experts == e)[None, :]).astype(BF)
        for e in range(experts)
    ]

    def to_slots(e, rows):
        spread = jnp.dot(placing[e], rows, preferred_element_type=F32).astype(BF)
        return spread.reshape(owners, capacity, width)

    def from_slots(parts):
        return sum(
            lax.dot_general(m, part, TN, preferred_element_type=F32)
            for m, part in zip(placing, parts)
        )

    upstream_half = own_half(cotangent.reshape(block, width))
    with scope("cot_out"):
        arrived_grad = spread_rows(
            jnp.stack([to_slots(e, upstream_half) for e in range(experts)], axis=1)
        )

    near_out, near_log = run_self_forward(projected, local)
    carried = ()
    for p in range(pairs):
        carried = run_cross_forward(p, word, projected, far[p], near_out, near_log, carried)
    context, log_rows = carried

    sent_half = lax.dot_general(other_half(context), output, NT, preferred_element_type=F32)
    kept_half = lax.dot_general(own_half(context), output, NT, preferred_element_type=F32)
    with scope("attended_tp"):
        received = swap(sent_half.astype(BF), "tp")
    resid = own_half(rows_in).astype(F32) + kept_half + received.astype(F32)
    second_rows, second_standard, second_spread = norm_input_rows(
        resid, layer_norm_gains[1], layer_norm_biases[1]
    )
    second = second_rows.astype(BF)
    arrived = []
    for e in range(experts):
        with scope(f"rows_out_{e}"):
            arrived.append(spread_rows(to_slots(e, second)).reshape(owners * capacity, width))

    returned, crossing = [], []
    carried = ()
    for e in range(experts):
        with scope(f"expert_{e}"):
            sent, small, rows_grad, gu, ku, gd, kd = run_expert(
                e, word, arrived[e], arrived_grad, ups, downs, vectors, carried
            )
        carried = (sent, small)
        with scope(f"rows_back_{e}"):
            returned.append(
                spread_rows(rows_grad.reshape(owners, capacity, width)).reshape(-1, width)
            )
        sums = []
        for name, give, keep in (("up", gu, ku), ("down", gd, kd)):
            dims = (2, thin, ff) if name == "up" else (2, cut, width)
            give, keep = give.reshape(dims), keep.reshape(dims)
            with scope(f"{name}_grad_tp_{e}"):
                sums.append((keep, swap(give, "tp")))
        crossing.append(sums)

    half_grad = from_slots(returned).astype(BF).astype(F32)
    norm_grad, gain_two, shift_two = norm_back(
        half_grad, second_standard, second_spread, layer_norm_gains[1]
    )
    attended_half = (upstream_half.astype(F32) + norm_grad).astype(BF)
    with scope("attended_grad_tp"):
        attended_grad = join_halves(attended_half)

    with scope("output_back"):
        sent = spread_rows(sent).transpose(1, 0, 2, 3).reshape(experts, owners * capacity, width)
    expert_half = from_slots([sent[e] for e in range(experts)])
    with scope("mixed_tp"):
        mixed = join_halves((resid + expert_half).astype(BF))

    def sum_owners(value):
        value = spread_rows(value.astype(BF).reshape(owners, -1, local))
        return jnp.sum(value.astype(F32), axis=0)

    context_grad = jnp.dot(attended_grad, output, preferred_element_type=F32).astype(BF)
    far_query, far_back = [], []
    for p in range(pairs):
        query, pair_grad = run_cross_backward(
            p, word, projected, far[p], context_grad, context, log_rows
        )
        far_query.append(query)
        with scope(f"far_back_{p}"):
            far_back.append(swap(pair_grad, "ctx"))
    projection_sums = []
    with scope("out_sum"):
        projection_sums.append(
            sum_owners(
                lax.dot_general(attended_grad, context, TN, preferred_element_type=F32)
            )
        )

    def cross_sum(e, at):
        keep, got = crossing[e][at]
        first_sum = (keep[0].astype(F32) + got[0].astype(F32)).astype(BF)
        if e:
            first_sum = after(first_sum, far_back[-2])
        with scope(f"grad_ctx_{e}_{at}"):
            crossed = swap(first_sum, "ctx")
        return keep[1].astype(F32) + got[1].astype(F32) + crossed.astype(F32)

    up_grad, down_grad = (
        jnp.stack([cross_sum(e, at) for e in range(experts)]) for at in range(2)
    )
    small = small + swap(small, "tp")
    small = small + swap(small, "ctx")
    quarter = place * 2 + side
    up_shift_grad = lax.dynamic_slice(small, (0, quarter * cut), (experts, cut))
    vectors_grad = lax.dynamic_slice(
        small[2].reshape(2 * experts, width), (0, quarter * thin), (2 * experts, thin)
    )

    grads = ()
    for p in range(pairs):
        grads = run_self_backward(
            p, projected, context_grad, context, log_rows, far_query[p], far_back[p], grads
        )
        pair = grads[:, 3 * PAIR * p : 3 * PAIR * (p + 1)]
        with scope(f"qkv_sum_{p}"):
            projection_sums.append(
                sum_owners(lax.dot_general(first, pair, TN, preferred_element_type=F32))
            )
        grads = (grads,)
    grads = grads[0]

    first_part = lax.dot_general(grads, project, NT, preferred_element_type=F32).astype(BF)
    with scope("first_tp"):
        first_grad = first_part.astype(F32) + swap(first_part, "tp").astype(F32)
    stream_grad, gain_one, shift_one = norm_back(
        first_grad, first_standard, first_spread, layer_norm_gains[0]
    )
    tokens_grad = attended_grad.astype(F32) + stream_grad

    sums = jnp.stack(projection_sums).reshape(1 + pairs, 2, -1, local)
    give = lax.dynamic_index_in_dim(sums, 1 - place, 1, keepdims=False).astype(BF)
    keep = lax.dynamic_index_in_dim(sums, place, 1, keepdims=False)
    with scope("sums_ctx"):
        total = keep + swap(give, "ctx").astype(F32)
    out_grad = total[0].T
    qkv_grad = total[1:].reshape(pairs, -1, 3, PAIR).transpose(2, 1, 0, 3).reshape(3, -1, local)

    two = jnp.stack([gain_two, shift_two])
    two = two + swap(two, "tp")
    norms = jnp.stack([gain_one, two[0], shift_one, two[1]]).reshape(4, owners, -1)
    norms = jnp.sum(spread_rows(norms.transpose(1, 0, 2)), axis=0)
    norms = norms + swap(norms, "ctx")
    piece = width // (2 * owners)
    norms = lax.dynamic_slice(norms, (0, place * piece), (4, piece))
    return (
        mixed.reshape(1, 1, block, width),
        tokens_grad.reshape(1, 1, block, width),
        qkv_grad,
        out_grad,
        norms[:2],
        norms[2:],
        up_grad,
        up_shift_grad,
        down_grad,
        vectors_grad[:experts],
        vectors_grad[experts:],
    )


def solution(mesh):
    paired = mesh.shape["ctx"] == 2 and mesh.shape["tp"] == 2
    in_specs = (
        P("fsdp", "ctx", None, None),
        P("fsdp", "ctx", None, None),
        P("fsdp", "ctx", "tp", None),
        P(None, "fsdp", "tp"),
        P("tp", "fsdp"),
        P(),
        P(),
        P("fsdp", ("ctx", "tp"), None),
        P("fsdp", ("ctx", "tp")),
        P("fsdp", ("ctx", "tp"), None),
        P("fsdp", ("ctx", "tp")),
        P("fsdp", ("ctx", "tp")),
    )
    out_specs = (
        P("fsdp", "ctx", None, None),
        P("fsdp", "ctx", None, None),
        P(None, ("fsdp", "ctx"), "tp"),
        P("tp", ("fsdp", "ctx")),
        P(None, ("fsdp", "ctx")),
        P(None, ("fsdp", "ctx")),
        P("fsdp", ("ctx", "tp"), None),
        P("fsdp", ("ctx", "tp")),
        P("fsdp", ("ctx", "tp"), None),
        P("fsdp", ("ctx", "tp")),
        P("fsdp", ("ctx", "tp")),
    )
    return jax.shard_map(
        shards_pair if paired else shards_any, mesh=mesh, in_specs=in_specs, out_specs=out_specs, check_vma=False)
```
